32 devices in a mesh: scen: 8 (over z, x), row: 2 (over y), col: 2 (over core).
Axes of the slice: x: 2, y: 2, z: 4, core: 2. Of those that a mesh axis runs over, the one named last changes fastest.
Arguments:
- coupling: bfloat16 [24, 512, 3072], P('scen', None, ('row', 'col')), may hold values from -0.078125 to 0.078125
- factor_inv: bfloat16 [24, 512, 512], P('scen'), as said below
- block_mask: int32 [24, 4, 24], P('scen', None, ('row', 'col')), may hold values 0 or 1
Outputs:
- schur: float32 [2, 1536, 2, 2, 768], P('row', 'scen', None, 'col')
The draws below stay inside these ranges and needn't reach their ends.
Inputs may be any that keep to these rules, and one draw needn't show every extreme that they name: factor_inv is lower triangular with a positive diagonal.
All inputs are finite; a program needn't handle non-finite values. No bound on the sum of `block_mask` on one device may be relied on, other than what follows from the above.
Results may differ from the reference program's by a relative error of at most 0.00064.
Values may be sent and summed in bfloat16 or wider, within the bound.
A program may use at most 64 MiB of HBM per device.

```python
import jax
import jax.numpy as jnp
from jax import lax

NB = 512
NS = 3072
BLK = 128
SCENS = 24
N_ROW = 2
N_COL = 2


def draw_factor_inv(key, part):
    first, second = jax.random.split(key)
    rows = jnp.arange(NB)[:, None]
    cols = jnp.arange(NB)[None, :]
    lower = (cols < rows).astype(jnp.float32)
    eye = (cols == rows).astype(jnp.float32)
    off = jax.random.normal(first, (SCENS, NB, NB), jnp.float32)
    diag = jax.random.uniform(second, (SCENS, NB, 1), jnp.float32, 0.5, 1.5)
    value = off * lower * NB ** (-0.5) + eye * diag
    return value.astype(jnp.bfloat16)


def touch_ends(entries, key, least, largest):
    spot = [jax.random.randint(jax.random.fold_in(key, axis), (), 0, length) for axis, length in enumerate(entries.shape)]
    longest = entries.shape.index(max(entries.shape))
    beside = spot[:longest] + [(spot[longest] + 1) % entries.shape[longest]] + spot[longest + 1:]
    return entries.at[tuple(spot)].set(least).at[tuple(beside)].set(largest)


def with_spikes(result, own_key, source, target, blocks, factor):
    owner, partner = [(jnp.arange(result.shape[position]) // (result.shape[position] // blocks)).reshape([-1 if axis == position else 1 for axis in range(result.ndim)]) for position in (source, target)]
    chosen = jax.random.permutation(own_key, blocks)[partner]
    strong = (owner == chosen) | (owner == (partner + blocks // 2) % blocks)
    return jnp.where(strong, factor * result, result)


def block_levels(rng, shape, shards, smallest, top_value):
    def one(position, parts):
        draws = jax.random.uniform(jax.random.fold_in(jax.random.fold_in(rng, 6), position), (parts,), jnp.float32, smallest / len(shards), top_value / len(shards))
        return jnp.repeat(jnp.exp(draws), shape[position] // parts).reshape((-1,) + (1,) * (len(shape) - position - 1))

    factor_of = one(*shards[0])
    for cut in shards[1:]:
        factor_of = factor_of * one(*cut)
    return factor_of


def heavy_noise(stream_key, dims, deviation, limit, cuts, heavy, held_as=jnp.bfloat16):
    entries = deviation * jax.random.normal(stream_key, dims, jnp.float32)
    if cuts:
        entries = entries * block_levels(stream_key, dims, cuts, -0.22, 0.18)
    return jnp.clip(with_spikes(entries, jax.random.fold_in(stream_key, 3), *heavy), -limit, limit).astype(held_as)


def setup_inputs(seed: int = 0) -> dict:
    splits = jax.random.split(jax.random.key(seed), 4)
    return {
        "coupling": heavy_noise(splits[0], (SCENS, NB, NS), (NB * SCENS) ** -0.5, 0.078125, ((0, 8), (2, 4)), (0, 2, 8, 2.0)),
        "factor_inv": draw_factor_inv(jax.random.fold_in(splits[3], 71), 0),
        "block_mask": touch_ends((jax.random.randint(splits[2], (SCENS, NB // BLK, NS // BLK), 0, 2) < 1).astype(jnp.int32), jax.random.fold_in(splits[2], 1), 0, 1),
    }


def reference(coupling, factor_inv, block_mask):
    def step(total, items):
        block, factor, pattern = items
        spread = jnp.broadcast_to(pattern[:, None, :, None], (NB // BLK, BLK, NS // BLK, BLK)).reshape(NB, NS)
        masked = block * spread.astype(jnp.bfloat16)
        solved = jnp.dot(factor, masked, preferred_element_type=jnp.float32).astype(jnp.bfloat16)
        product = lax.dot_general(solved, solved, (((0,), (0,)), ((), ())), preferred_element_type=jnp.float32)
        return total + product, None

    start = jnp.zeros((NS, NS), jnp.float32)
    total, unused = lax.scan(step, start, (coupling, factor_inv, block_mask))
    return total.reshape(N_ROW, NS // N_ROW, N_ROW, N_COL, NS // (N_ROW * N_COL))
```

```python
import functools

import jax
import jax.numpy as jnp
from jax import lax
from jax.experimental import pallas as pl
from jax.experimental.pallas import tpu as pltpu
from jax.sharding import PartitionSpec as P

BLK = 128
LANES = 128
HEAD = 16
LINK = jnp.int16
FINE = 64.0
TOP = 14.9
PIECE = 256
DEPTH = 4
MESH = pl.DeviceIdType.MESH
NT = (((1,), (1,)), ((), ()))
ORDER = (2, 1, 3, 0)


def encode(value):
    most = jnp.maximum(jnp.max(jnp.abs(value), axis=0, keepdims=True), 1e-30)
    power = jnp.ceil(jnp.log2(most) * FINE)
    scaled = jnp.round(value * jnp.exp2(TOP - power / FINE))
    head = jnp.broadcast_to(power, (HEAD, value.shape[1]))
    return head.astype(jnp.int32).astype(LINK), scaled.astype(jnp.int32).astype(LINK)


def decode(head, scaled):
    power = head.astype(jnp.int32).astype(jnp.float32)[0:1, :]
    return scaled.astype(jnp.int32).astype(jnp.float32) * jnp.exp2(power / FINE - TOP)


def pieces_of(width):
    early = [(0, base, PIECE) for base in range(0, width, PIECE)]
    late = [(1, base, PIECE) for base in range(0, width - PIECE, PIECE)]
    late += [(1, width - PIECE, PIECE // 2), (1, width - PIECE // 2, PIECE // 2)]
    return early, late


def kernel(coupling, factor, mask, out, c_in, f_in, own, left, right,
           in_sem, col_send, col_recv, row_send, row_recv,
           x_send, x_recv, z_send, z_recv, away, *buffers):
    groups, order, width = coupling.shape
    share = 2 * width // (2 * DEPTH)
    early, late = pieces_of(width)
    pieces = early + late
    count = len(pieces)
    keep, x_out, x_in, z_out, z_in = [buffers[i * count:(i + 1) * count] for i in range(5)]
    scen, row, col = lax.axis_index("scen"), lax.axis_index("row"), lax.axis_index("col")
    z, x = scen // 2, lax.rem(scen, 2)
    across = (2 * z + 1 - x, row, col)
    opposite = (scen, 1 - row, col)
    sibling = (scen, row, 1 - col)

    def level(d):
        return lax.rem(z + d, DEPTH)

    loads = []
    for g in range(groups):
        for src, dst, k in ((coupling, c_in, 0), (factor, f_in, 1)):
            load = pltpu.make_async_copy(src.at[g], dst.at[g], in_sem.at[g, k])
            load.start()
            loads.append(load)

    barrier = pltpu.get_barrier_semaphore()
    peers = [across, opposite, sibling] + [(2 * level(d) + x, row, col) for d in range(1, DEPTH)]
    for peer in peers:
        pl.semaphore_signal(barrier, inc=1, device_id=peer, device_id_type=MESH)

    copies = []

    def send(src, dst, send_sem, recv_sem, device):
        copy = pltpu.make_async_remote_copy(
            src_ref=src, dst_ref=dst, send_sem=send_sem, recv_sem=recv_sem,
            device_id=device, device_id_type=MESH)
        copy.start()
        copies.append(copy)
        return copy

    col_copies, row_copies = [], {}

    def send_row(k, g):
        _, base, w = late[k]
        row_copies[k, g] = send(
            own.at[g, pl.ds(base, w)], right.at[g, pl.ds(base, w)],
            row_send.at[k, g], row_recv.at[k, g], opposite)

    half = width // 2
    for g in range(groups):
        loads[2 * g].wait()
        loads[2 * g + 1].wait()
        rows = []
        for i in range(order // BLK):
            rows.append(jnp.concatenate([
                c_in[g, i * BLK:(i + 1) * BLK, j * BLK:(j + 1) * BLK]
                * mask[g, i, j].astype(jnp.float32).astype(jnp.bfloat16)
                for j in range(width // BLK)], axis=1))
        masked = jnp.concatenate(rows, axis=0)
        solved = jnp.dot(f_in[g], masked, preferred_element_type=jnp.float32)
        turned = solved.T.astype(jnp.bfloat16)
        own[g] = turned
        for a in range(2):
            for b in range(2):
                at = pl.multiple_of(col * half + a * share, share)
                left[g, b, pl.ds(at, share), :] = turned[(2 * a + b) * share:(2 * a + b + 1) * share]
        if g == 0:
            pl.semaphore_wait(barrier, len(peers))
        send_row(0, g)
        for b in range(2):
            mine = left.at[g, b, pl.ds(pl.multiple_of(col * half, half), half)]
            col_copies.append(send(mine, mine, col_send.at[g, b], col_recv.at[g, b], sibling))
    for k in range(1, len(late)):
        for g in range(groups):
            send_row(k, g)

    def product(b, p):
        kind, base, w = pieces[p]
        source = right if kind else own
        total = None
        for g in range(groups):
            term = lax.dot_general(
                left[g, b], source[g, base:base + w, :], NT, preferred_element_type=jnp.float32)
            total = term if total is None else total + term
        return total

    def slab(d):
        return pl.ds(pl.multiple_of(level(d) * share, share), share)

    def pack(ref, value):
        head, scaled = encode(value)
        ref[0:HEAD, :] = head
        ref[HEAD:, :] = scaled

    def unpack(ref):
        return decode(ref[0:HEAD, :], ref[HEAD:, :])

    x_copies, z_copies = {}, {}

    def multiply(p):
        kind, base, w = pieces[p]
        if kind:
            for g in range(groups):
                row_copies[late.index(pieces[p]), g].wait_recv()
        away[:, 0:w] = product(1 - x, p)
        for d in ORDER:
            pack(x_out[p].at[d], away[slab(d), 0:w])
            x_copies[p, d] = send(x_out[p].at[d], x_in[p].at[d], x_send.at[p, d], x_recv.at[p, d], across)
        keep[p][...] = product(x, p)

    def pass_on(p):
        for d in ORDER:
            x_copies[p, d].wait_recv()
            value = keep[p][slab(d), :] + unpack(x_in[p].at[d])
            if d == 0:
                keep[p][slab(0), :] = value
            else:
                pack(z_out[p].at[d - 1], value)
                z_copies[p, d] = send(
                    z_out[p].at[d - 1], z_in[p].at[d - 1], z_send.at[p, d - 1], z_recv.at[p, d - 1],
                    (2 * level(d) + x, row, col))

    def finish(p):
        kind, base, w = pieces[p]
        value = keep[p][slab(0), :]
        for d in range(1, DEPTH):
            z_copies[p, d].wait_recv()
            value += unpack(z_in[p].at[d - 1])
        lines = width // LANES
        place = (1 - row if kind else row) * lines + base // LANES
        for c in range(w // LANES):
            out[pl.ds(place + c, share, stride=2 * lines), :] = value[:, c * LANES:(c + 1) * LANES]

    for copy in col_copies:
        copy.wait_recv()
    plan = [(multiply, 0), (multiply, 1), (multiply, 2), (pass_on, 0), (pass_on, 1), (multiply, 3),
            (pass_on, 2), (finish, 0), (finish, 1), (multiply, 4), (pass_on, 3), (finish, 2),
            (multiply, 5), (pass_on, 4), (finish, 3), (multiply, 6), (pass_on, 5), (pass_on, 6),
            (finish, 4), (finish, 5), (finish, 6)]
    for task, p in plan:
        task(p)
    for copy in copies:
        copy.wait_send()


def fused(coupling, factor_inv, block_mask):
    groups, order, width = coupling.shape
    share = 2 * width // (2 * DEPTH)
    early, late = pieces_of(width)
    pieces = early + late
    count = len(pieces)
    hbm = pl.BlockSpec(memory_space=pl.ANY)
    message = HEAD + share
    tile = pl.pallas_call(
        kernel,
        out_shape=jax.ShapeDtypeStruct((share * 2 * width // LANES, LANES), jnp.float32),
        in_specs=[hbm, hbm, pl.BlockSpec(memory_space=pltpu.SMEM)],
        out_specs=pl.BlockSpec(memory_space=pltpu.VMEM),
        scratch_shapes=[
            pltpu.VMEM((groups, order, width), jnp.bfloat16),
            pltpu.VMEM((groups, order, order), jnp.bfloat16),
            pltpu.VMEM((groups, width, order), jnp.bfloat16),
            pltpu.VMEM((groups, 2, width, order), jnp.bfloat16),
            pltpu.VMEM((groups, width, order), jnp.bfloat16),
            pltpu.SemaphoreType.DMA((groups, 2)),
            pltpu.SemaphoreType.DMA((groups, 2)),
            pltpu.SemaphoreType.DMA((groups, 2)),
            pltpu.SemaphoreType.DMA((len(late), groups)),
            pltpu.SemaphoreType.DMA((len(late), groups)),
            pltpu.SemaphoreType.DMA((count, DEPTH)),
            pltpu.SemaphoreType.DMA((count, DEPTH)),
            pltpu.SemaphoreType.DMA((count, DEPTH - 1)),
            pltpu.SemaphoreType.DMA((count, DEPTH - 1)),
            pltpu.VMEM((width, PIECE), jnp.float32),
            *[pltpu.VMEM((width, w), jnp.float32) for _, _, w in pieces],
            *[pltpu.VMEM((DEPTH, message, w), LINK) for _, _, w in pieces],
            *[pltpu.VMEM((DEPTH, message, w), LINK) for _, _, w in pieces],
            *[pltpu.VMEM((DEPTH - 1, message, w), LINK) for _, _, w in pieces],
            *[pltpu.VMEM((DEPTH - 1, message, w), LINK) for _, _, w in pieces],
        ],
        compiler_params=pltpu.CompilerParams(
            collective_id=0, has_side_effects=True, vmem_limit_bytes=60 * 1024 * 1024),
    )(coupling, factor_inv, block_mask)
    return tile.reshape(1, share, 2, 1, width)


def plain(coupling, factor_inv, block_mask):
    groups, order, width = coupling.shape
    spread = jnp.broadcast_to(
        block_mask[:, :, None, :, None], (groups, order // BLK, BLK, width // BLK, BLK)
    )
    masked = coupling * spread.reshape(groups, order, width).astype(jnp.bfloat16)
    solved = jnp.einsum(
        "snk,skw->snw", factor_inv, masked, preferred_element_type=jnp.float32
    ).astype(jnp.bfloat16)
    left = lax.all_gather(solved, "col", axis=2, tiled=True)
    share = left.shape[2] // lax.axis_size("scen")
    tile = lax.dot_general(
        left,
        lax.all_gather(solved, "row", axis=2, tiled=True),
        (((0, 1), (0, 1)), ((), ())),
        preferred_element_type=jnp.float32,
    )
    summed = lax.psum_scatter(tile, "scen", scatter_dimension=0, tiled=True)
    return summed.reshape(1, share, summed.shape[1] // width, 1, width)


def solution(mesh):
    n, n_row = mesh.shape["scen"], mesh.shape["row"]

    def shards(coupling, factor_inv, block_mask):
        groups, order, width = coupling.shape
        if n == 2 * DEPTH and n_row == 2 and width == 3 * PIECE and order % BLK == 0 and groups <= 4:
            return fused(coupling, factor_inv, block_mask)
        return plain(coupling, factor_inv, block_mask)

    in_specs = (
        P("scen", None, ("row", "col")),
        P("scen", None, None),
        P("scen", None, ("row", "col")),
    )
    out_specs = P("row", "scen", None, "col", None)
    return jax.shard_map(shards, mesh=mesh, in_specs=in_specs, out_specs=out_specs, check_vma=False)
```

```python
import functools

import jax
import jax.numpy as jnp
from jax import lax
from jax.experimental import pallas as pl
from jax.experimental.pallas import tpu as pltpu
from jax.sharding import PartitionSpec as P

BLK = 128
LANES = 128
HEAD = 16
LINK = jnp.int16
FINE = 64.0
TOP = 14.9
DEPTH = 4
MESH = pl.DeviceIdType.MESH
NT = (((1,), (1,)), ((), ()))
PIECES = ((0, 3), (0, 2), (1, DEPTH), (1, DEPTH))
SWAPS = ((0, 1), (0, 2), (1, 1), (2, 0), (3, 0))
GROUPS = ((0, (0,)), (0, (1, 2)), (1, (1,)), (2, (3, 2)), (2, (1, 0)), (3, (3,)), (3, (2,)), (3, (1,)), (3, (0,)), (1, (0,)))


def power_of(values):
    most = jnp.max(jnp.abs(values[0]), axis=0, keepdims=True)
    for value in values[1:]:
        most = jnp.maximum(most, jnp.max(jnp.abs(value), axis=0, keepdims=True))
    return jnp.ceil(jnp.log2(jnp.maximum(most, 1e-30)) * FINE)


def pack(ref, values):
    power = power_of(values)
    scale = jnp.exp2(TOP - power / FINE)
    ref[0:HEAD, :] = jnp.broadcast_to(power, (HEAD, power.shape[1])).astype(jnp.int32).astype(LINK)
    start = HEAD
    for value in values:
        count = value.shape[0]
        ref[start:start + count, :] = jnp.round(value * scale).astype(jnp.int32).astype(LINK)
        start += count


def unpack(ref, start, count):
    power = ref[0:HEAD, :].astype(jnp.int32).astype(jnp.float32)[0:1, :]
    scaled = ref[HEAD + start:HEAD + start + count, :].astype(jnp.int32).astype(jnp.float32)
    return scaled * jnp.exp2(power / FINE - TOP)


def keys_of():
    keys = [(p, e) for p, (_, size) in enumerate(PIECES) for e in range(size)]
    return {key: i for i, key in enumerate(keys)}


def when(condition, action):
    if condition is True:
        action()
    elif condition is not False:
        pl.when(condition)(action)


def kernel(coupling, factor, mask, out, c_in, f_in, own, left, right, keep, away, joined,
           z_out, near_in, far_in, swap_out, swap_in,
           in_sem, col_send, col_recv, row_send, row_recv, x_send, x_recv,
           near_recv, far_recv, z_send, swap_send, swap_recv, *buffers):
    groups, order, width = coupling.shape
    depth = groups * order
    part = depth // 2
    share = width // DEPTH
    block = 2 * share
    lines = width // LANES
    wide = block // LANES
    x_out, x_in = buffers[:len(GROUPS)], buffers[len(GROUPS):]
    scen, row, col = lax.axis_index("scen"), lax.axis_index("row"), lax.axis_index("col")
    z, x = scen // 2, lax.rem(scen, 2)
    near = z + 1 - 2 * lax.rem(z, 2)
    far = lax.rem(z + 2, DEPTH)
    last = DEPTH - 1 - z
    apart = (z, near, far, last)
    across = (2 * z + 1 - x, row, col)
    opposite = (scen, 1 - row, col)
    sibling = (scen, row, 1 - col)
    index = keys_of()

    turn = [jnp.where(row == 0, groups - 1 - g, g) for g in range(groups)]
    loads = []
    for g in range(groups):
        pair = []
        for src, dst, k in ((coupling, c_in, 0), (factor, f_in, 1)):
            load = pltpu.make_async_copy(src.at[turn[g]], dst.at[g], in_sem.at[g, k])
            load.start()
            pair.append(load)
        loads.append(pair)

    barrier = pltpu.get_barrier_semaphore()
    peers = [across, opposite, sibling] + [(2 * level + x, row, col) for level in apart[1:]]
    for peer in peers:
        pl.semaphore_signal(barrier, inc=1, device_id=peer, device_id_type=MESH)

    pending = []

    def remote(src, dst, send_sem, recv_sem, device, condition=True):
        copy = pltpu.make_async_remote_copy(
            src_ref=src, dst_ref=dst, send_sem=send_sem, recv_sem=recv_sem,
            device_id=device, device_id_type=MESH)
        pending.append((copy, condition))
        return copy

    col_copies, row_copies = [], {}

    def send_row(half, chunk):
        if chunk == 0:
            size, start, to = order, jnp.where(row == 0, depth - order, 0), jnp.where(row == 0, part - order, 0)
        else:
            size, start, to = part - order, jnp.where(row == 0, part, order), jnp.where(row == 0, 0, order)
        rows = pl.ds(half * block, block)
        copy = remote(
            own.at[rows, pl.ds(pl.multiple_of(start, 256), size)],
            right.at[rows, pl.ds(pl.multiple_of(to, 256), size)],
            row_send.at[half, chunk], row_recv.at[half, chunk], opposite)
        copy.start()
        back = pltpu.make_async_copy(
            right.at[rows, pl.ds(pl.multiple_of(part - size - to, 256), size)],
            right.at[rows, pl.ds(pl.multiple_of(part - size - to, 256), size)], row_recv.at[half, chunk])
        row_copies[half, chunk] = back

    for g in range(groups):
        for load in loads[g]:
            load.wait()
        rows = []
        for i in range(order // BLK):
            rows.append(jnp.concatenate([
                c_in[g, i * BLK:(i + 1) * BLK, j * BLK:(j + 1) * BLK]
                * mask[turn[g], i, j].astype(jnp.float32).astype(jnp.bfloat16)
                for j in range(width // BLK)], axis=1))
        masked = jnp.concatenate(rows, axis=0)
        solved = jnp.dot(f_in[g], masked, preferred_element_type=jnp.float32)
        turned = solved.T.astype(jnp.bfloat16)
        lanes = pl.ds(pl.multiple_of(turn[g] * order, order), order)
        own[:, lanes] = turned
        for a in range(2):
            for b in range(2):
                at = pl.multiple_of(col * block + a * share, share)
                left[b, pl.ds(at, share), lanes] = turned[(2 * a + b) * share:(2 * a + b + 1) * share]
        if g == 0:
            pl.semaphore_wait(barrier, len(peers))
            send_row(0, 0)
        elif g == 1:
            send_row(0, 1)
            send_row(1, 0)
            send_row(1, 1)
        mine = left.at[:, pl.ds(pl.multiple_of(col * block, block), block), lanes]
        copy = remote(mine, mine, col_send.at[g], col_recv.at[g], sibling)
        copy.start()
        col_copies.append(copy)

    def column(p):
        return (3 * col, 1 + col, 2 * col, 2 * col + 1)[p]

    def level(p, e):
        return apart[e] if PIECES[p][0] else lax.rem(column(p) + e, DEPTH)

    def product(b, p, e):
        rows = pl.ds(pl.multiple_of(level(p, e) * share, share), share)
        if PIECES[p][0]:
            lhs = left[b, rows, pl.ds(pl.multiple_of(row * part, 256), part)]
            rhs = right[(p - 2) * block:(p - 1) * block, :]
        else:
            lhs = left[b, rows, :]
            rhs = own[pl.ds(pl.multiple_of((col if p == 0 else 1 - col) * block, block), block), :]
        return lax.dot_general(lhs, rhs, NT, preferred_element_type=jnp.float32)

    place_of = {(p, e): (k, i) for k, (p, es) in enumerate(GROUPS) for i, e in enumerate(es)}
    x_copies, near_copies, far_copies, swaps = {}, {}, {}, {}

    def multiply(k):
        p, es = GROUPS[k]
        for i, e in enumerate(es):
            away[i] = product(1 - x, p, e)
        pack(x_out[k], [away[i] for i in range(len(es))])
        copy = remote(x_out[k], x_in[k], x_send.at[k], x_recv.at[k], across)
        copy.start()
        x_copies[k] = copy

    def retain(k):
        p, es = GROUPS[k]
        for e in es:
            keep[index[p, e]] = product(x, p, e)

    def roles(p, e):
        if PIECES[p][0]:
            return e == 0, e % 2 == 1, e == 2
        at = level(p, e)
        return z == at, lax.rem(z + at, 2) == 1, far == at

    def direct(p):
        return p == 3

    def take(p, e):
        k, i = place_of[p, e]
        if i == 0:
            x_copies[k].wait_recv()
        me = index[p, e]
        final, differ, relay = roles(p, e)
        keep[me] = keep[me] + unpack(x_in[k], i * share, share)
        if direct(p):
            if e:
                pack(z_out.at[me], [keep[me]])
                copy = remote(z_out.at[me], near_in.at[me], z_send.at[me], near_recv.at[me],
                              (2 * level(p, e) + x, row, col))
                copy.start()
                near_copies[p, e] = copy
            return
        to = index[p, e - 1] if PIECES[p][0] and e % 2 else me
        copy = remote(z_out.at[me], near_in.at[to], z_send.at[me], near_recv.at[to],
                      (2 * near + x, row, col), differ)
        near_copies[p, e] = copy if to == me else pltpu.make_async_copy(
            near_in.at[to], near_in.at[to], near_recv.at[to])
        if PIECES[p][0] and e % 2 == 0:
            pending.pop()

        def go():
            pack(z_out.at[me], [keep[me]])
            copy.start()

        when(differ, go)

    def relay(p, e):
        if direct(p):
            return
        me = index[p, e]
        final, differ, relayed = roles(p, e)
        if differ is True:
            return
        same = (not differ) if isinstance(differ, bool) else jnp.logical_not(differ)
        arrived = pltpu.make_async_copy(near_in.at[me], near_in.at[me], near_recv.at[me])
        to = index[p, 0] if PIECES[p][0] else me
        copy = None
        if relayed is not False:
            copy = remote(z_out.at[me], far_in.at[to], z_send.at[me], far_recv.at[to],
                          (2 * far + x, row, col), relayed)

        def add():
            arrived.wait()
            keep[me] = keep[me] + unpack(near_in.at[me], 0, share)

        when(same, add)
        if copy is not None:
            def go():
                pack(z_out.at[me], [keep[me]])
                copy.start()

            when(relayed, go)

    def show(place, value):
        for c in range(wide):
            out[pl.ds(place + c, share, stride=2 * lines), :] = value[:, c * LANES:(c + 1) * LANES]

    def finish(p, e):
        kind = PIECES[p][0]
        me = index[p, e]
        final = roles(p, e)[0]
        at = level(p, e)
        copies = []
        if (p, e) in SWAPS:
            s = SWAPS.index((p, e))
            side = 1 - row if kind else row
            for b in range(2):
                copies.append(remote(
                    swap_out.at[s, b], swap_in.at[kind, lax.rem(at, 2), x],
                    swap_send.at[s, b], swap_recv.at[kind, lax.rem(at, 2), x],
                    (2 * column(p) + b, side, at // 2), final))

        def go():
            if direct(p):
                for d in range(1, DEPTH):
                    other = index[p, d]
                    near_copies[p, d].wait_recv()
                    keep[me] = keep[me] + unpack(near_in.at[other], 0, share)
            else:
                pltpu.make_async_copy(far_in.at[me], far_in.at[me], far_recv.at[me]).wait()
                keep[me] = keep[me] + unpack(far_in.at[me], 0, share)
            if copies:
                flipped = keep[me].T
                for b, copy in enumerate(copies):
                    pack(swap_out.at[s, b], [flipped[b * share:(b + 1) * share, :]])
                    copy.start()
            if not kind:
                show(row * lines + (column(p) - 2 * col) * wide, keep[me])

        when(final, go)

    def swapped(kind, l):
        for b in range(2):
            pltpu.make_async_copy(swap_in.at[kind, l, b], swap_in.at[kind, l, b], swap_recv.at[kind, l, b]).wait()
            joined[:, b * share:(b + 1) * share] = unpack(swap_in.at[kind, l, b], 0, share)

    def close(kind, l):
        if kind:
            swapped(1, l)
            show((1 - row) * lines + l * wide, joined[...] + keep[index[2 + l, 0]])
            return
        steps = lax.rem(z - (2 * col + l) + DEPTH, DEPTH)
        absent = steps > jnp.where(col == l, 2, 1)

        def go():
            swapped(0, l)
            show(row * lines + l * wide, joined[...])

        when(absent, go)

    def arrive(half):
        for chunk in range(2):
            row_copies[half, chunk].wait()

    for copy in col_copies:
        copy.wait_recv()
    plan = [(multiply, 0), (multiply, 1), (retain, 0), (retain, 1), (multiply, 2), (retain, 2),
            (take, 0, 0), (arrive, 0), (multiply, 3), (multiply, 4), (relay, 0, 0), (take, 0, 1), (take, 0, 2),
            (retain, 3), (retain, 4), (take, 1, 1), (relay, 0, 1), (relay, 0, 2), (finish, 0, 0),
            (relay, 1, 1), (take, 2, 3), (take, 2, 2), (finish, 0, 1), (finish, 0, 2), (arrive, 1),
            (multiply, 5), (multiply, 6), (multiply, 7), (multiply, 8), (multiply, 9),
            (finish, 1, 1), (relay, 2, 2), (retain, 5), (retain, 6), (retain, 7), (retain, 8), (retain, 9),
            (take, 2, 1), (take, 2, 0), (relay, 2, 0), (close, 0, 0), (close, 0, 1),
            (take, 3, 3), (finish, 2, 0), (take, 3, 2), (take, 3, 1), (take, 3, 0), (take, 1, 0),
            (close, 1, 0), (relay, 1, 0), (finish, 3, 0), (finish, 1, 0), (close, 1, 1)]
    for task, *which in plan:
        task(*which)
    for copy, condition in pending:
        when(condition, copy.wait_send)


def fused(coupling, factor_inv, block_mask):
    groups, order, width = coupling.shape
    depth, share = groups * order, width // DEPTH
    block, message, count = 2 * share, HEAD + share, len(keys_of())
    hbm = pl.BlockSpec(memory_space=pl.ANY)
    packets = [pltpu.VMEM((HEAD + share * len(es), block), LINK) for _, es in GROUPS]
    tile = pl.pallas_call(
        kernel,
        out_shape=jax.ShapeDtypeStruct((share * 2 * width // LANES, LANES), jnp.float32),
        in_specs=[hbm, hbm, pl.BlockSpec(memory_space=pltpu.SMEM)],
        out_specs=pl.BlockSpec(memory_space=pltpu.VMEM),
        scratch_shapes=[
            pltpu.VMEM((groups, order, width), jnp.bfloat16),
            pltpu.VMEM((groups, order, order), jnp.bfloat16),
            pltpu.VMEM((width, depth), jnp.bfloat16),
            pltpu.VMEM((2, width, depth), jnp.bfloat16),
            pltpu.VMEM((width, depth // 2), jnp.bfloat16),
            pltpu.VMEM((count, share, block), jnp.float32),
            pltpu.VMEM((2, share, block), jnp.float32),
            pltpu.VMEM((share, block), jnp.float32),
            pltpu.VMEM((count, message, block), LINK),
            pltpu.VMEM((count, message, block), LINK),
            pltpu.VMEM((count, message, block), LINK),
            pltpu.VMEM((len(SWAPS), 2, message, share), LINK),
            pltpu.VMEM((2, 2, 2, message, share), LINK),
            pltpu.SemaphoreType.DMA((groups, 2)),
            pltpu.SemaphoreType.DMA((groups,)),
            pltpu.SemaphoreType.DMA((groups,)),
            pltpu.SemaphoreType.DMA((2, 2)),
            pltpu.SemaphoreType.DMA((2, 2)),
            pltpu.SemaphoreType.DMA((len(GROUPS),)),
            pltpu.SemaphoreType.DMA((len(GROUPS),)),
            pltpu.SemaphoreType.DMA((count,)),
            pltpu.SemaphoreType.DMA((count,)),
            pltpu.SemaphoreType.DMA((count,)),
            pltpu.SemaphoreType.DMA((len(SWAPS), 2)),
            pltpu.SemaphoreType.DMA((2, 2, 2)),
            *packets, *packets,
        ],
        compiler_params=pltpu.CompilerParams(
            collective_id=0, has_side_effects=True, vmem_limit_bytes=52 * 1024 * 1024),
    )(coupling, factor_inv, block_mask)
    return tile.reshape(1, share, 2, 1, width)


def plain(coupling, factor_inv, block_mask):
    groups, order, width = coupling.shape
    spread = jnp.broadcast_to(
        block_mask[:, :, None, :, None], (groups, order // BLK, BLK, width // BLK, BLK)
    )
    masked = coupling * spread.reshape(groups, order, width).astype(jnp.bfloat16)
    solved = jnp.einsum(
        "snk,skw->snw", factor_inv, masked, preferred_element_type=jnp.float32
    ).astype(jnp.bfloat16)
    left = lax.all_gather(solved, "col", axis=2, tiled=True)
    share = left.shape[2] // lax.axis_size("scen")
    tile = lax.dot_general(
        left,
        lax.all_gather(solved, "row", axis=2, tiled=True),
        (((0, 1), (0, 1)), ((), ())),
        preferred_element_type=jnp.float32,
    )
    summed = lax.psum_scatter(tile, "scen", scatter_dimension=0, tiled=True)
    return summed.reshape(1, share, summed.shape[1] // width, 1, width)


def solution(mesh):
    n, n_row = mesh.shape["scen"], mesh.shape["row"]

    def shards(coupling, factor_inv, block_mask):
        groups, order, width = coupling.shape
        if n == 2 * DEPTH and n_row == 2 and (groups, order, width) == (3, 512, 768):
            return fused(coupling, factor_inv, block_mask)
        return plain(coupling, factor_inv, block_mask)

    in_specs = (
        P("scen", None, ("row", "col")),
        P("scen", None, None),
        P("scen", None, ("row", "col")),
    )
    out_specs = P("row", "scen", None, "col", None)
    return jax.shard_map(shards, mesh=mesh, in_specs=in_specs, out_specs=out_specs, check_vma=False)
```

```python
import functools

import jax
import jax.numpy as jnp
from jax import lax
from jax.experimental import pallas as pl
from jax.experimental.pallas import tpu as pltpu
from jax.sharding import PartitionSpec as P

BLK = 128
LANES = 128
HEAD = 16
LINK = jnp.int16
FINE = 64.0
TOP = 14.9
DEPTH = 4
MESH = pl.DeviceIdType.MESH
NT = (((1,), (1,)), ((), ()))
PIECES = (3, 2)
LATE = ((0, 256), (256, 256), (512, 128), (640, 128))
SWAPS = ((0, 1), (0, 2), (1, 1))
GROUPS = ((0, (0,)), (0, (1, 2)), (1, (1,)), (1, (0,)))
LATE_GROUPS = ((0, (3, 2)), (0, (1, 0)), (1, (3, 2)), (1, (1, 0)), (2, (3, 2)), (2, (1, 0)),
               (3, (3,)), (3, (2,)), (3, (1,)), (3, (0,)))
ORDER = (3, 2, 1, 0)


def power_of(values):
    most = jnp.max(jnp.abs(values[0]), axis=0, keepdims=True)
    for value in values[1:]:
        most = jnp.maximum(most, jnp.max(jnp.abs(value), axis=0, keepdims=True))
    return jnp.ceil(jnp.log2(jnp.maximum(most, 1e-30)) * FINE)


def pack(ref, values):
    power = power_of(values)
    scale = jnp.exp2(TOP - power / FINE)
    ref[0:HEAD, :] = jnp.broadcast_to(power, (HEAD, power.shape[1])).astype(jnp.int32).astype(LINK)
    start = HEAD
    for value in values:
        count = value.shape[0]
        ref[start:start + count, :] = jnp.round(value * scale).astype(jnp.int32).astype(LINK)
        start += count


def unpack(ref, start, count):
    power = ref[0:HEAD, :].astype(jnp.int32).astype(jnp.float32)[0:1, :]
    scaled = ref[HEAD + start:HEAD + start + count, :].astype(jnp.int32).astype(jnp.float32)
    return scaled * jnp.exp2(power / FINE - TOP)


def pack_square(ref, value):
    side = value.shape[0]
    power = power_of([value])
    scaled = jnp.round(value * jnp.exp2(TOP - power / FINE))
    heads = (power[:, :LANES], jnp.concatenate([power[:, LANES:]] * 2, axis=1))
    rest = jnp.concatenate([scaled[:side // 2, LANES:], scaled[side // 2:, LANES:]], axis=1)
    start = 0
    for head, body in zip(heads, (scaled[:, :LANES], rest)):
        ref[start:start + HEAD, :] = jnp.broadcast_to(head, (HEAD, LANES)).astype(jnp.int32).astype(LINK)
        ref[start + HEAD:start + HEAD + body.shape[0], :] = body.astype(jnp.int32).astype(LINK)
        start += HEAD + body.shape[0]


def unpack_square(ref, to, base, side):
    to[:, base:base + LANES] = unpack(ref, 0, side)
    rest = unpack(ref.at[HEAD + side:], 0, side // 2)
    more = side - LANES
    to[0:side // 2, base + LANES:base + side] = rest[:, :more]
    to[side // 2:, base + LANES:base + side] = rest[:, more:]


INDEX = {key: i for i, key in enumerate((p, e) for p, size in enumerate(PIECES) for e in range(size))}


def kernel(coupling, factor, mask, out, c_in, f_in, own, left, right, away, keep, joined,
           z_out, near_in, far_in, swap_out, swap_in,
           in_sem, col_send, col_recv, row_send, row_recv, x_send, x_recv, lx_send, lx_recv,
           z_send, near_recv, far_recv, swap_send, swap_recv, lz_send, lz_recv, *buffers):
    groups, order, width = coupling.shape
    share = width // DEPTH
    block = 2 * share
    lines = width // LANES
    sizes = (len(GROUPS), len(GROUPS), len(LATE_GROUPS), len(LATE_GROUPS), len(LATE), len(LATE), len(LATE))
    parts, start = [], 0
    for size in sizes:
        parts.append(buffers[start:start + size])
        start += size
    x_out, x_in, lx_out, lx_in, l_keep, lz_out, lz_in = parts
    scen, row, col = lax.axis_index("scen"), lax.axis_index("row"), lax.axis_index("col")
    z, x = scen // 2, lax.rem(scen, 2)
    near = z + 1 - 2 * lax.rem(z, 2)
    far = lax.rem(z + 2, DEPTH)
    apart = (z, near, far, DEPTH - 1 - z)
    across = (2 * z + 1 - x, row, col)
    opposite = (scen, 1 - row, col)
    sibling = (scen, row, 1 - col)

    loads = []
    for g in range(groups):
        pair = []
        for src, dst, k in ((coupling, c_in, 0), (factor, f_in, 1)):
            load = pltpu.make_async_copy(src.at[g], dst.at[g], in_sem.at[g, k])
            load.start()
            pair.append(load)
        loads.append(pair)

    barrier = pltpu.get_barrier_semaphore()
    peers = [across, opposite, sibling] + [(2 * level + x, row, col) for level in apart[1:]]
    for peer in peers:
        pl.semaphore_signal(barrier, inc=1, device_id=peer, device_id_type=MESH)

    pending = []

    def remote(src, dst, send_sem, recv_sem, device, condition=None):
        copy = pltpu.make_async_remote_copy(
            src_ref=src, dst_ref=dst, send_sem=send_sem, recv_sem=recv_sem,
            device_id=device, device_id_type=MESH)
        pending.append((copy, condition))
        if condition is None:
            copy.start()
        return copy

    col_copies, row_copies = [], {}

    def send_row(k, g, count):
        base, w = LATE[k]
        rows, lanes = pl.ds(base, w), pl.ds(g * order, count * order)
        row_copies[k, g] = remote(
            own.at[rows, lanes], right.at[rows, lanes], row_send.at[k, g], row_recv.at[k, g], opposite)

    for g in range(groups):
        for load in loads[g]:
            load.wait()
        rows = []
        for i in range(order // BLK):
            rows.append(jnp.concatenate([
                c_in[g, i * BLK:(i + 1) * BLK, j * BLK:(j + 1) * BLK]
                * mask[g, i, j].astype(jnp.float32).astype(jnp.bfloat16)
                for j in range(width // BLK)], axis=1))
        masked = jnp.concatenate(rows, axis=0)
        solved = jnp.dot(f_in[g], masked, preferred_element_type=jnp.float32)
        turned = solved.T.astype(jnp.bfloat16)
        lanes = slice(g * order, (g + 1) * order)
        own[:, lanes] = turned
        if g == 0:
            pl.semaphore_wait(barrier, len(peers))
        send_row(0, g, 1)
        for a in range(2):
            for b in range(2):
                at = pl.multiple_of(col * block + a * share, share)
                left[b, pl.ds(at, share), lanes] = turned[(2 * a + b) * share:(2 * a + b + 1) * share]
        mine = left.at[:, pl.ds(pl.multiple_of(col * block, block), block), pl.ds(g * order, order)]
        col_copies.append(remote(mine, mine, col_send.at[g], col_recv.at[g], sibling))
    for k in range(1, len(LATE)):
        send_row(k, 0, groups)

    def column(p):
        return 3 * col if p == 0 else 1 + col

    def level(p, e):
        return lax.rem(column(p) + e, DEPTH)

    def slab(at):
        return pl.ds(pl.multiple_of(at * share, share), share)

    def product(b, p, e):
        rhs = own[pl.ds(pl.multiple_of((col if p == 0 else 1 - col) * block, block), block), :]
        return lax.dot_general(left[b, slab(level(p, e)), :], rhs, NT, preferred_element_type=jnp.float32)

    def late_product(b, p, d):
        base, w = LATE[p]
        return lax.dot_general(left[b, slab(apart[d]), :], right[base:base + w, :], NT,
                               preferred_element_type=jnp.float32)

    x_copies, lx_copies, lz_copies = {}, {}, {}
    place_of = {(p, e): (k, i) for k, (p, es) in enumerate(GROUPS) for i, e in enumerate(es)}
    late_place = {(p, d): (k, i) for k, (p, ds) in enumerate(LATE_GROUPS) for i, d in enumerate(ds)}

    def multiply(k):
        p, es = GROUPS[k]
        for i, e in enumerate(es):
            away[i] = product(1 - x, p, e)
        pack(x_out[k], [away[i] for i in range(len(es))])
        x_copies[k] = remote(x_out[k], x_in[k], x_send.at[k], x_recv.at[k], across)

    def retain(k):
        p, es = GROUPS[k]
        for e in es:
            keep[INDEX[p, e]] = product(x, p, e)

    def take(p, e):
        k, i = place_of[p, e]
        if i == 0:
            x_copies[k].wait_recv()
        me, at = INDEX[p, e], level(p, e)
        differ = lax.rem(z + at, 2) == 1
        copy = remote(z_out.at[me], near_in.at[me], z_send.at[me], near_recv.at[me], (2 * near + x, row, col), differ)
        keep[me] = keep[me] + unpack(x_in[k], i * share, share)

        @pl.when(differ)
        def _():
            pack(z_out.at[me], [keep[me]])
            copy.start()

    def relay(p, e):
        me, at = INDEX[p, e], level(p, e)
        passed = far == at
        copy = remote(z_out.at[me], far_in.at[me], z_send.at[me], far_recv.at[me], (2 * far + x, row, col), passed)

        @pl.when(lax.rem(z + at, 2) == 0)
        def _():
            pltpu.make_async_copy(near_in.at[me], near_in.at[me], near_recv.at[me]).wait()
            keep[me] = keep[me] + unpack(near_in.at[me], 0, share)

        @pl.when(passed)
        def _():
            pack(z_out.at[me], [keep[me]])
            copy.start()

    def show(place, value):
        for c in range(value.shape[1] // LANES):
            out[pl.ds(place + c, share, stride=2 * lines), :] = value[:, c * LANES:(c + 1) * LANES]

    def finish(p, e):
        me, at = INDEX[p, e], level(p, e)
        final = z == at
        copies = []
        if (p, e) in SWAPS:
            s = SWAPS.index((p, e))
            for b in range(2):
                copies.append(remote(
                    swap_out.at[s, b], swap_in.at[lax.rem(at, 2), x],
                    swap_send.at[s, b], swap_recv.at[lax.rem(at, 2), x],
                    (2 * column(p) + b, row, at // 2), final))

        @pl.when(final)
        def _():
            pltpu.make_async_copy(far_in.at[me], far_in.at[me], far_recv.at[me]).wait()
            keep[me] = keep[me] + unpack(far_in.at[me], 0, share)
            if copies:
                flipped = keep[me].T
                for b, copy in enumerate(copies):
                    pack_square(swap_out.at[s, b], flipped[b * share:(b + 1) * share, :])
                    copy.start()
            show(row * lines + (column(p) - 2 * col) * (block // LANES), keep[me])

    def close(l):
        steps = lax.rem(z - (2 * col + l) + DEPTH, DEPTH)

        @pl.when(steps > jnp.where(col == l, 2, 1))
        def _():
            for b in range(2):
                pltpu.make_async_copy(swap_in.at[l, b], swap_in.at[l, b], swap_recv.at[l, b]).wait()
                unpack_square(swap_in.at[l, b], joined, b * share, share)
            show(row * lines + l * (block // LANES), joined[...])

    def gather():
        for copy in col_copies:
            copy.wait_recv()

    def arrive(p):
        for g in range(groups if p == 0 else 1):
            row_copies[p, g].wait_recv()

    def late_multiply(k):
        p, ds = LATE_GROUPS[k]
        w = LATE[p][1]
        for i, d in enumerate(ds):
            away[i, :, 0:w] = late_product(1 - x, p, d)
        pack(lx_out[k], [away[i, :, 0:w] for i in range(len(ds))])
        lx_copies[k] = remote(lx_out[k], lx_in[k], lx_send.at[k], lx_recv.at[k], across)

    def late_retain(p):
        for d in ORDER:
            l_keep[p][d] = late_product(x, p, d)

    def late_take(p, d):
        k, i = late_place[p, d]
        if i == 0:
            lx_copies[k].wait_recv()
        value = l_keep[p][d] + unpack(lx_in[k], i * share, share)
        if d == 0:
            l_keep[p][0] = value
            return
        pack(lz_out[p].at[d], [value])
        lz_copies[p, d] = remote(
            lz_out[p].at[d], lz_in[p].at[d], lz_send.at[p, d], lz_recv.at[p, d], (2 * apart[d] + x, row, col))

    def late_finish(p):
        value = l_keep[p][0]
        for d in ORDER[:-1]:
            lz_copies[p, d].wait_recv()
            value += unpack(lz_in[p].at[d], 0, share)
        show((1 - row) * lines + LATE[p][0] // LANES, value)

    plan = [(multiply, 0), (gather,), (multiply, 1), (multiply, 2), (multiply, 3),
            (retain, 0), (retain, 1), (retain, 2), (retain, 3),
            (take, 0, 0), (take, 0, 1), (take, 0, 2), (relay, 0, 0), (arrive, 0),
            (late_multiply, 0), (late_multiply, 1), (late_retain, 0),
            (take, 1, 1), (relay, 0, 1), (relay, 0, 2), (finish, 0, 0), (finish, 0, 1), (finish, 0, 2),
            (take, 1, 0), (relay, 1, 1), (relay, 1, 0), (finish, 1, 1),
            (late_take, 0, 3), (late_take, 0, 2), (finish, 1, 0), (late_take, 0, 1), (late_take, 0, 0),
            (close, 0), (close, 1), (arrive, 1), (late_multiply, 2), (late_multiply, 3), (late_retain, 1), (late_finish, 0),
            (late_take, 1, 3), (late_take, 1, 2), (arrive, 2), (late_multiply, 4), (late_multiply, 5), (late_retain, 2),
            (late_take, 1, 1), (late_take, 1, 0), (late_take, 2, 3), (late_take, 2, 2), (arrive, 3),
            (late_multiply, 6), (late_multiply, 7), (late_multiply, 8), (late_multiply, 9),
            (late_take, 2, 1), (late_take, 2, 0), (late_retain, 3), (late_finish, 1),
            (late_take, 3, 3), (late_take, 3, 2), (late_finish, 2), (late_take, 3, 1), (late_take, 3, 0), (late_finish, 3)]
    for task, *which in plan:
        task(*which)
    for copy, condition in pending:
        if condition is None:
            copy.wait_send()
        else:
            pl.when(condition)(copy.wait_send)


def fused(coupling, factor_inv, block_mask):
    groups, order, width = coupling.shape
    depth, share = groups * order, width // DEPTH
    block, message, count = 2 * share, HEAD + share, len(INDEX)
    square = 2 * HEAD + share + share // 2
    hbm = pl.BlockSpec(memory_space=pl.ANY)
    packets = [pltpu.VMEM((HEAD + share * len(es), block), LINK) for _, es in GROUPS]
    late_packets = [pltpu.VMEM((HEAD + share * len(ds), LATE[p][1]), LINK) for p, ds in LATE_GROUPS]
    sums = [pltpu.VMEM((DEPTH, share, w), jnp.float32) for _, w in LATE]
    messages = [pltpu.VMEM((DEPTH, message, w), LINK) for _, w in LATE]
    dma = pltpu.SemaphoreType.DMA
    tile = pl.pallas_call(
        kernel,
        out_shape=jax.ShapeDtypeStruct((share * 2 * width // LANES, LANES), jnp.float32),
        in_specs=[hbm, hbm, pl.BlockSpec(memory_space=pltpu.SMEM)],
        out_specs=pl.BlockSpec(memory_space=pltpu.VMEM),
        scratch_shapes=[
            pltpu.VMEM((groups, order, width), jnp.bfloat16),
            pltpu.VMEM((groups, order, order), jnp.bfloat16),
            pltpu.VMEM((width, depth), jnp.bfloat16),
            pltpu.VMEM((2, width, depth), jnp.bfloat16),
            pltpu.VMEM((width, depth), jnp.bfloat16),
            pltpu.VMEM((2, share, block), jnp.float32),
            pltpu.VMEM((count, share, block), jnp.float32),
            pltpu.VMEM((share, block), jnp.float32),
            pltpu.VMEM((count, message, block), LINK),
            pltpu.VMEM((count, message, block), LINK),
            pltpu.VMEM((count, message, block), LINK),
            pltpu.VMEM((len(SWAPS), 2, square, LANES), LINK),
            pltpu.VMEM((2, 2, square, LANES), LINK),
            dma((groups, 2)), dma((groups,)), dma((groups,)),
            dma((len(LATE), groups)), dma((len(LATE), groups)),
            dma((len(GROUPS),)), dma((len(GROUPS),)),
            dma((len(LATE_GROUPS),)), dma((len(LATE_GROUPS),)),
            dma((count,)), dma((count,)), dma((count,)),
            dma((len(SWAPS), 2)), dma((2, 2)),
            dma((len(LATE), DEPTH)), dma((len(LATE), DEPTH)),
            *packets, *packets, *late_packets, *late_packets, *sums, *messages, *messages,
        ],
        compiler_params=pltpu.CompilerParams(
            collective_id=0, has_side_effects=True, vmem_limit_bytes=52 * 1024 * 1024),
    )(coupling, factor_inv, block_mask)
    return tile.reshape(1, share, 2, 1, width)


def plain(coupling, factor_inv, block_mask):
    groups, order, width = coupling.shape
    spread = jnp.broadcast_to(
        block_mask[:, :, None, :, None], (groups, order // BLK, BLK, width // BLK, BLK)
    )
    masked = coupling * spread.reshape(groups, order, width).astype(jnp.bfloat16)
    solved = jnp.einsum(
        "snk,skw->snw", factor_inv, masked, preferred_element_type=jnp.float32
    ).astype(jnp.bfloat16)
    left = lax.all_gather(solved, "col", axis=2, tiled=True)
    share = left.shape[2] // lax.axis_size("scen")
    tile = lax.dot_general(
        left,
        lax.all_gather(solved, "row", axis=2, tiled=True),
        (((0, 1), (0, 1)), ((), ())),
        preferred_element_type=jnp.float32,
    )
    summed = lax.psum_scatter(tile, "scen", scatter_dimension=0, tiled=True)
    return summed.reshape(1, share, summed.shape[1] // width, 1, width)


def solution(mesh):
    n, n_row = mesh.shape["scen"], mesh.shape["row"]

    def shards(coupling, factor_inv, block_mask):
        groups, order, width = coupling.shape
        if n == 2 * DEPTH and n_row == 2 and (groups, order, width) == (3, 512, 768):
            return fused(coupling, factor_inv, block_mask)
        return plain(coupling, factor_inv, block_mask)

    in_specs = (
        P("scen", None, ("row", "col")),
        P("scen", None, None),
        P("scen", None, ("row", "col")),
    )
    out_specs = P("row", "scen", None, "col", None)
    return jax.shard_map(shards, mesh=mesh, in_specs=in_specs, out_specs=out_specs, check_vma=False)
```

```python
import functools

import jax
import jax.numpy as jnp
from jax import lax
from jax.experimental import pallas as pl
from jax.experimental.pallas import tpu as pltpu
from jax.sharding import PartitionSpec as P

BLK = 128
LANES = 128
HEAD = 16
LINK = jnp.int16
FINE = 64.0
TOP = 14.9
DEPTH = 4
MESH = pl.DeviceIdType.MESH
NT = (((1,), (1,)), ((), ()))
PIECES = (3, 2)
LATE = ((0, 256), (256, 256), (512, 128), (640, 128))
SWAPS = ((0, 1), (0, 2), (1, 1))
GROUPS = ((0, (0,)), (0, (1, 2)), (1, (1,)), (1, (0,)))
LATE_GROUPS = ((0, (3, 2)), (0, (1, 0)), (1, (3, 2)), (1, (1, 0)), (2, (3, 2)), (2, (1, 0)),
               (3, (3,)), (3, (2,)), (3, (1,)), (3, (0,)))
ORDER = (3, 2, 1, 0)


def power_of(values):
    most = jnp.max(jnp.abs(values[0]), axis=0, keepdims=True)
    for value in values[1:]:
        most = jnp.maximum(most, jnp.max(jnp.abs(value), axis=0, keepdims=True))
    return jnp.ceil(jnp.log2(jnp.maximum(most, 1e-30)) * FINE)


def pack(ref, values):
    power = power_of(values)
    scale = jnp.exp2(TOP - power / FINE)
    ref[0:HEAD, :] = jnp.broadcast_to(power, (HEAD, power.shape[1])).astype(jnp.int32).astype(LINK)
    start = HEAD
    for value in values:
        count = value.shape[0]
        ref[start:start + count, :] = jnp.round(value * scale).astype(jnp.int32).astype(LINK)
        start += count


def unpack(ref, start, count):
    power = ref[0:HEAD, :].astype(jnp.int32).astype(jnp.float32)[0:1, :]
    scaled = ref[HEAD + start:HEAD + start + count, :].astype(jnp.int32).astype(jnp.float32)
    return scaled * jnp.exp2(power / FINE - TOP)


def pack_square(ref, value):
    side = value.shape[0]
    power = power_of([value])
    scaled = jnp.round(value * jnp.exp2(TOP - power / FINE))
    heads = (power[:, :LANES], jnp.concatenate([power[:, LANES:]] * 2, axis=1))
    rest = jnp.concatenate([scaled[:side // 2, LANES:], scaled[side // 2:, LANES:]], axis=1)
    start = 0
    for head, body in zip(heads, (scaled[:, :LANES], rest)):
        ref[start:start + HEAD, :] = jnp.broadcast_to(head, (HEAD, LANES)).astype(jnp.int32).astype(LINK)
        ref[start + HEAD:start + HEAD + body.shape[0], :] = body.astype(jnp.int32).astype(LINK)
        start += HEAD + body.shape[0]


def unpack_square(ref, to, base, side):
    to[:, base:base + LANES] = unpack(ref, 0, side)
    rest = unpack(ref.at[HEAD + side:], 0, side // 2)
    more = side - LANES
    to[0:side // 2, base + LANES:base + side] = rest[:, :more]
    to[side // 2:, base + LANES:base + side] = rest[:, more:]


INDEX = {key: i for i, key in enumerate((p, e) for p, size in enumerate(PIECES) for e in range(size))}


def kernel(coupling, factor, mask, out, c_in, f_in, own, left, right, away, keep, joined,
           z_out, near_in, far_in, swap_out, swap_in,
           in_sem, col_send, col_recv, row_send, row_recv, x_send, x_recv, lx_send, lx_recv,
           z_send, near_recv, far_recv, swap_send, swap_recv, lz_send, lz_recv, *buffers):
    groups, order, width = coupling.shape
    share = width // DEPTH
    block = 2 * share
    lines = width // LANES
    sizes = (len(GROUPS), len(GROUPS), len(LATE_GROUPS), len(LATE_GROUPS), len(LATE), len(LATE), len(LATE))
    parts, start = [], 0
    for size in sizes:
        parts.append(buffers[start:start + size])
        start += size
    x_out, x_in, lx_out, lx_in, l_keep, lz_out, lz_in = parts
    scen, row, col = lax.axis_index("scen"), lax.axis_index("row"), lax.axis_index("col")
    z, x = scen // 2, lax.rem(scen, 2)
    near = z + 1 - 2 * lax.rem(z, 2)
    far = lax.rem(z + 2, DEPTH)
    apart = (z, near, far, DEPTH - 1 - z)
    across = (2 * z + 1 - x, row, col)
    opposite = (scen, 1 - row, col)
    sibling = (scen, row, 1 - col)

    loads = []
    for g in range(groups):
        pair = []
        for src, dst, k in ((coupling, c_in, 0), (factor, f_in, 1)):
            load = pltpu.make_async_copy(src.at[g], dst.at[g], in_sem.at[g, k])
            load.start()
            pair.append(load)
        loads.append(pair)

    barrier = pltpu.get_barrier_semaphore()
    peers = [across, opposite, sibling] + [(2 * level + x, row, col) for level in apart[1:]]
    for peer in peers:
        pl.semaphore_signal(barrier, inc=1, device_id=peer, device_id_type=MESH)

    pending = []

    def remote(src, dst, send_sem, recv_sem, device, condition=None):
        copy = pltpu.make_async_remote_copy(
            src_ref=src, dst_ref=dst, send_sem=send_sem, recv_sem=recv_sem,
            device_id=device, device_id_type=MESH)
        pending.append((copy, condition))
        if condition is None:
            copy.start()
        return copy

    col_copies, row_copies = [], {}

    def send_row(k, g, count):
        base, w = LATE[k]
        rows, lanes = pl.ds(base, w), pl.ds(g * order, count * order)
        row_copies[k, g] = remote(
            own.at[rows, lanes], right.at[rows, lanes], row_send.at[k, g], row_recv.at[k, g], opposite)

    for g in range(groups):
        for load in loads[g]:
            load.wait()
        rows = []
        for i in range(order // BLK):
            rows.append(jnp.concatenate([
                c_in[g, i * BLK:(i + 1) * BLK, j * BLK:(j + 1) * BLK]
                * mask[g, i, j].astype(jnp.float32).astype(jnp.bfloat16)
                for j in range(width // BLK)], axis=1))
        masked = jnp.concatenate(rows, axis=0)
        solved = jnp.dot(f_in[g], masked, preferred_element_type=jnp.float32)
        turned = solved.T.astype(jnp.bfloat16)
        lanes = slice(g * order, (g + 1) * order)
        own[:, lanes] = turned
        if g == 0:
            pl.semaphore_wait(barrier, len(peers))
        send_row(0, g, 1)
        for a in range(2):
            for b in range(2):
                at = pl.multiple_of(col * block + a * share, share)
                left[b, pl.ds(at, share), lanes] = turned[(2 * a + b) * share:(2 * a + b + 1) * share]
        mine = left.at[:, pl.ds(pl.multiple_of(col * block, block), block), pl.ds(g * order, order)]
        col_copies.append(remote(mine, mine, col_send.at[g], col_recv.at[g], sibling))
    for k in range(1, len(LATE)):
        send_row(k, 0, groups)

    def column(p):
        return 3 * col if p == 0 else 1 + col

    def level(p, e):
        return lax.rem(column(p) + e, DEPTH)

    def slab(at):
        return pl.ds(pl.multiple_of(at * share, share), share)

    def product(b, p, e):
        rhs = own[pl.ds(pl.multiple_of((col if p == 0 else 1 - col) * block, block), block), :]
        return lax.dot_general(left[b, slab(level(p, e)), :], rhs, NT, preferred_element_type=jnp.float32)

    def late_product(b, p, d):
        base, w = LATE[p]
        return lax.dot_general(left[b, slab(apart[d]), :], right[base:base + w, :], NT,
                               preferred_element_type=jnp.float32)

    x_copies, lx_copies, lz_copies = {}, {}, {}
    place_of = {(p, e): (k, i) for k, (p, es) in enumerate(GROUPS) for i, e in enumerate(es)}
    late_place = {(p, d): (k, i) for k, (p, ds) in enumerate(LATE_GROUPS) for i, d in enumerate(ds)}

    def multiply(k):
        p, es = GROUPS[k]
        for i, e in enumerate(es):
            away[i] = product(1 - x, p, e)
        pack(x_out[k], [away[i] for i in range(len(es))])
        x_copies[k] = remote(x_out[k], x_in[k], x_send.at[k], x_recv.at[k], across)

    def retain(k):
        p, es = GROUPS[k]
        for e in es:
            keep[INDEX[p, e]] = product(x, p, e)

    def take(p, e):
        k, i = place_of[p, e]
        if i == 0:
            x_copies[k].wait_recv()
        me, at = INDEX[p, e], level(p, e)
        differ = lax.rem(z + at, 2) == 1
        copy = remote(z_out.at[me], near_in.at[me], z_send.at[me], near_recv.at[me], (2 * near + x, row, col), differ)
        keep[me] = keep[me] + unpack(x_in[k], i * share, share)

        @pl.when(differ)
        def _():
            pack(z_out.at[me], [keep[me]])
            copy.start()

    def relay(p, e):
        me, at = INDEX[p, e], level(p, e)
        passed = far == at
        copy = remote(z_out.at[me], far_in.at[me], z_send.at[me], far_recv.at[me], (2 * far + x, row, col), passed)

        @pl.when(lax.rem(z + at, 2) == 0)
        def _():
            pltpu.make_async_copy(near_in.at[me], near_in.at[me], near_recv.at[me]).wait()
            keep[me] = keep[me] + unpack(near_in.at[me], 0, share)

        @pl.when(passed)
        def _():
            pack(z_out.at[me], [keep[me]])
            copy.start()

    def show(place, value):
        for c in range(value.shape[1] // LANES):
            out[pl.ds(place + c, share, stride=2 * lines), :] = value[:, c * LANES:(c + 1) * LANES]

    def finish(p, e):
        me, at = INDEX[p, e], level(p, e)
        final = z == at
        copies = []
        if (p, e) in SWAPS:
            s = SWAPS.index((p, e))
            for b in range(2):
                copies.append(remote(
                    swap_out.at[s, b], swap_in.at[lax.rem(at, 2), x],
                    swap_send.at[s, b], swap_recv.at[lax.rem(at, 2), x],
                    (2 * column(p) + b, row, at // 2), final))

        @pl.when(final)
        def _():
            pltpu.make_async_copy(far_in.at[me], far_in.at[me], far_recv.at[me]).wait()
            keep[me] = keep[me] + unpack(far_in.at[me], 0, share)
            if copies:
                flipped = keep[me].T
                for b, copy in enumerate(copies):
                    pack_square(swap_out.at[s, b], flipped[b * share:(b + 1) * share, :])
                    copy.start()
            show(row * lines + (column(p) - 2 * col) * (block // LANES), keep[me])

    def close(l):
        steps = lax.rem(z - (2 * col + l) + DEPTH, DEPTH)

        @pl.when(steps > jnp.where(col == l, 2, 1))
        def _():
            for b in range(2):
                pltpu.make_async_copy(swap_in.at[l, b], swap_in.at[l, b], swap_recv.at[l, b]).wait()
                unpack_square(swap_in.at[l, b], joined, b * share, share)
            show(row * lines + l * (block // LANES), joined[...])

    def gather():
        for copy in col_copies:
            copy.wait_recv()

    def arrive(p):
        for g in range(groups if p == 0 else 1):
            row_copies[p, g].wait_recv()

    def late_multiply(k):
        p, ds = LATE_GROUPS[k]
        w = LATE[p][1]
        for i, d in enumerate(ds):
            away[i, :, 0:w] = late_product(1 - x, p, d)
        pack(lx_out[k], [away[i, :, 0:w] for i in range(len(ds))])
        lx_copies[k] = remote(lx_out[k], lx_in[k], lx_send.at[k], lx_recv.at[k], across)

    def late_retain(p):
        for d in ORDER:
            l_keep[p][d] = late_product(x, p, d)

    def late_take(p, d):
        k, i = late_place[p, d]
        if i == 0:
            lx_copies[k].wait_recv()
        value = l_keep[p][d] + unpack(lx_in[k], i * share, share)
        if d == 0:
            l_keep[p][0] = value
            return
        pack(lz_out[p].at[d], [value])
        lz_copies[p, d] = remote(
            lz_out[p].at[d], lz_in[p].at[d], lz_send.at[p, d], lz_recv.at[p, d], (2 * apart[d] + x, row, col))

    def late_finish(p):
        value = l_keep[p][0]
        for d in ORDER[:-1]:
            lz_copies[p, d].wait_recv()
            value += unpack(lz_in[p].at[d], 0, share)
        show((1 - row) * lines + LATE[p][0] // LANES, value)

    plan = [(multiply, 0), (gather,), (multiply, 1), (multiply, 2), (multiply, 3), (retain, 0), (retain, 1),
            (retain, 2), (retain, 3), (take, 0, 0), (take, 0, 1), (take, 0, 2), (relay, 0, 0), (arrive, 0),
            (late_multiply, 0), (late_multiply, 1), (late_retain, 0), (take, 1, 1), (relay, 0, 1), (relay, 0, 2),
            (finish, 0, 0), (finish, 0, 1), (finish, 0, 2), (late_take, 0, 3), (late_take, 0, 2), (take, 1, 0),
            (relay, 1, 1), (relay, 1, 0), (arrive, 1), (late_multiply, 2), (late_multiply, 3), (late_take, 0, 1),
            (late_take, 0, 0), (late_retain, 1), (late_finish, 0), (finish, 1, 1), (finish, 1, 0), (late_take, 1, 3),
            (arrive, 2), (late_multiply, 4), (late_multiply, 5), (late_take, 1, 2), (late_retain, 2),
            (late_take, 1, 1), (late_take, 1, 0), (late_take, 2, 3), (late_take, 2, 2), (close, 0), (close, 1),
            (arrive, 3), (late_multiply, 6), (late_multiply, 7), (late_multiply, 8), (late_multiply, 9),
            (late_take, 2, 1), (late_take, 2, 0), (late_retain, 3), (late_take, 3, 3), (late_take, 3, 2),
            (late_finish, 1), (late_finish, 2), (late_take, 3, 1), (late_take, 3, 0), (late_finish, 3)]
    for task, *which in plan:
        task(*which)
    for copy, condition in pending:
        if condition is None:
            copy.wait_send()
        else:
            pl.when(condition)(copy.wait_send)


def fused(coupling, factor_inv, block_mask):
    groups, order, width = coupling.shape
    depth, share = groups * order, width // DEPTH
    block, message, count = 2 * share, HEAD + share, len(INDEX)
    square = 2 * HEAD + share + share // 2
    hbm = pl.BlockSpec(memory_space=pl.ANY)
    packets = [pltpu.VMEM((HEAD + share * len(es), block), LINK) for _, es in GROUPS]
    late_packets = [pltpu.VMEM((HEAD + share * len(ds), LATE[p][1]), LINK) for p, ds in LATE_GROUPS]
    sums = [pltpu.VMEM((DEPTH, share, w), jnp.float32) for _, w in LATE]
    messages = [pltpu.VMEM((DEPTH, message, w), LINK) for _, w in LATE]
    dma = pltpu.SemaphoreType.DMA
    tile = pl.pallas_call(
        kernel,
        out_shape=jax.ShapeDtypeStruct((share * 2 * width // LANES, LANES), jnp.float32),
        in_specs=[hbm, hbm, pl.BlockSpec(memory_space=pltpu.SMEM)],
        out_specs=pl.BlockSpec(memory_space=pltpu.VMEM),
        scratch_shapes=[
            pltpu.VMEM((groups, order, width), jnp.bfloat16),
            pltpu.VMEM((groups, order, order), jnp.bfloat16),
            pltpu.VMEM((width, depth), jnp.bfloat16),
            pltpu.VMEM((2, width, depth), jnp.bfloat16),
            pltpu.VMEM((width, depth), jnp.bfloat16),
            pltpu.VMEM((2, share, block), jnp.float32),
            pltpu.VMEM((count, share, block), jnp.float32),
            pltpu.VMEM((share, block), jnp.float32),
            pltpu.VMEM((count, message, block), LINK),
            pltpu.VMEM((count, message, block), LINK),
            pltpu.VMEM((count, message, block), LINK),
            pltpu.VMEM((len(SWAPS), 2, square, LANES), LINK),
            pltpu.VMEM((2, 2, square, LANES), LINK),
            dma((groups, 2)), dma((groups,)), dma((groups,)),
            dma((len(LATE), groups)), dma((len(LATE), groups)),
            dma((len(GROUPS),)), dma((len(GROUPS),)),
            dma((len(LATE_GROUPS),)), dma((len(LATE_GROUPS),)),
            dma((count,)), dma((count,)), dma((count,)),
            dma((len(SWAPS), 2)), dma((2, 2)),
            dma((len(LATE), DEPTH)), dma((len(LATE), DEPTH)),
            *packets, *packets, *late_packets, *late_packets, *sums, *messages, *messages,
        ],
        compiler_params=pltpu.CompilerParams(
            collective_id=0, has_side_effects=True, vmem_limit_bytes=52 * 1024 * 1024),
    )(coupling, factor_inv, block_mask)
    return tile.reshape(1, share, 2, 1, width)


def plain(coupling, factor_inv, block_mask):
    groups, order, width = coupling.shape
    spread = jnp.broadcast_to(
        block_mask[:, :, None, :, None], (groups, order // BLK, BLK, width // BLK, BLK)
    )
    masked = coupling * spread.reshape(groups, order, width).astype(jnp.bfloat16)
    solved = jnp.einsum(
        "snk,skw->snw", factor_inv, masked, preferred_element_type=jnp.float32
    ).astype(jnp.bfloat16)
    left = lax.all_gather(solved, "col", axis=2, tiled=True)
    share = left.shape[2] // lax.axis_size("scen")
    tile = lax.dot_general(
        left,
        lax.all_gather(solved, "row", axis=2, tiled=True),
        (((0, 1), (0, 1)), ((), ())),
        preferred_element_type=jnp.float32,
    )
    summed = lax.psum_scatter(tile, "scen", scatter_dimension=0, tiled=True)
    return summed.reshape(1, share, summed.shape[1] // width, 1, width)


def solution(mesh):
    n, n_row = mesh.shape["scen"], mesh.shape["row"]

    def shards(coupling, factor_inv, block_mask):
        groups, order, width = coupling.shape
        if n == 2 * DEPTH and n_row == 2 and (groups, order, width) == (3, 512, 768):
            return fused(coupling, factor_inv, block_mask)
        return plain(coupling, factor_inv, block_mask)

    in_specs = (
        P("scen", None, ("row", "col")),
        P("scen", None, None),
        P("scen", None, ("row", "col")),
    )
    out_specs = P("row", "scen", None, "col", None)
    return jax.shard_map(shards, mesh=mesh, in_specs=in_specs, out_specs=out_specs, check_vma=False)
```

```python
import functools

import jax
import jax.numpy as jnp
from jax import lax
from jax.experimental import pallas as pl
from jax.experimental.pallas import tpu as pltpu
from jax.sharding import PartitionSpec as P

BLK = 128
LANES = 128
HEAD = 16
LINK = jnp.int16
FINE = 64.0
TOP = 14.9
DEPTH = 4
MESH = pl.DeviceIdType.MESH
NT = (((1,), (1,)), ((), ()))
PIECES = (3, 2)
LATE = ((0, 256), (256, 256), (512, 128), (640, 128))
SWAPS = ((0, 1), (0, 2), (1, 1))
GROUPS = ((0, (0,)), (0, (1, 2)), (1, (1,)), (1, (0,)))
LATE_GROUPS = ((0, (3, 2)), (0, (1, 0)), (1, (3, 2)), (1, (1, 0)), (2, (3, 2)), (2, (1, 0)),
               (3, (3,)), (3, (2,)), (3, (1,)), (3, (0,)))
ORDER = (3, 2, 1, 0)


def power_of(values):
    most = jnp.max(jnp.abs(values[0]), axis=0, keepdims=True)
    for value in values[1:]:
        most = jnp.maximum(most, jnp.max(jnp.abs(value), axis=0, keepdims=True))
    return jnp.ceil(jnp.log2(jnp.maximum(most, 1e-30)) * FINE)


def pack(ref, values):
    power = power_of(values)
    scale = jnp.exp2(TOP - power / FINE)
    ref[0:HEAD, :] = jnp.broadcast_to(power, (HEAD, power.shape[1])).astype(jnp.int32).astype(LINK)
    start = HEAD
    for value in values:
        count = value.shape[0]
        ref[start:start + count, :] = jnp.round(value * scale).astype(jnp.int32).astype(LINK)
        start += count


def unpack(ref, start, count):
    power = ref[0:HEAD, :].astype(jnp.int32).astype(jnp.float32)[0:1, :]
    scaled = ref[HEAD + start:HEAD + start + count, :].astype(jnp.int32).astype(jnp.float32)
    return scaled * jnp.exp2(power / FINE - TOP)


def pack_square(ref, value):
    side = value.shape[0]
    power = power_of([value])
    scaled = jnp.round(value * jnp.exp2(TOP - power / FINE))
    heads = (power[:, :LANES], jnp.concatenate([power[:, LANES:]] * 2, axis=1))
    rest = jnp.concatenate([scaled[:side // 2, LANES:], scaled[side // 2:, LANES:]], axis=1)
    start = 0
    for head, body in zip(heads, (scaled[:, :LANES], rest)):
        ref[start:start + HEAD, :] = jnp.broadcast_to(head, (HEAD, LANES)).astype(jnp.int32).astype(LINK)
        ref[start + HEAD:start + HEAD + body.shape[0], :] = body.astype(jnp.int32).astype(LINK)
        start += HEAD + body.shape[0]


def unpack_square(ref, to, base, side):
    to[:, base:base + LANES] = unpack(ref, 0, side)
    rest = unpack(ref.at[HEAD + side:], 0, side // 2)
    more = side - LANES
    to[0:side // 2, base + LANES:base + side] = rest[:, :more]
    to[side // 2:, base + LANES:base + side] = rest[:, more:]


INDEX = {key: i for i, key in enumerate((p, e) for p, size in enumerate(PIECES) for e in range(size))}


def kernel(coupling, factor, mask, out, c_in, f_in, own, left, right, away, keep, joined,
           z_out, near_in, far_in, swap_out, swap_in,
           in_sem, col_send, col_recv, row_send, row_recv, x_send, x_recv, lx_send, lx_recv,
           z_send, near_recv, far_recv, swap_send, swap_recv, lz_send, lz_recv, *buffers):
    groups, order, width = coupling.shape
    share = width // DEPTH
    block = 2 * share
    lines = width // LANES
    sizes = (len(GROUPS), len(GROUPS), len(LATE_GROUPS), len(LATE_GROUPS), len(LATE), len(LATE), len(LATE))
    parts, start = [], 0
    for size in sizes:
        parts.append(buffers[start:start + size])
        start += size
    x_out, x_in, lx_out, lx_in, l_keep, lz_out, lz_in = parts
    scen, row, col = lax.axis_index("scen"), lax.axis_index("row"), lax.axis_index("col")
    z, x = scen // 2, lax.rem(scen, 2)
    near = z + 1 - 2 * lax.rem(z, 2)
    far = lax.rem(z + 2, DEPTH)
    apart = (z, near, far, DEPTH - 1 - z)
    across = (2 * z + 1 - x, row, col)
    opposite = (scen, 1 - row, col)
    sibling = (scen, row, 1 - col)

    loads = []
    for g in range(groups):
        pair = []
        for src, dst, k in ((coupling, c_in, 0), (factor, f_in, 1)):
            load = pltpu.make_async_copy(src.at[g], dst.at[g], in_sem.at[g, k])
            load.start()
            pair.append(load)
        loads.append(pair)

    barrier = pltpu.get_barrier_semaphore()
    peers = [across, opposite, sibling] + [(2 * level + x, row, col) for level in apart[1:]]
    for peer in peers:
        pl.semaphore_signal(barrier, inc=1, device_id=peer, device_id_type=MESH)

    pending = []

    def remote(src, dst, send_sem, recv_sem, device, condition=None):
        copy = pltpu.make_async_remote_copy(
            src_ref=src, dst_ref=dst, send_sem=send_sem, recv_sem=recv_sem,
            device_id=device, device_id_type=MESH)
        pending.append((copy, condition))
        if condition is None:
            copy.start()
        return copy

    col_copies, row_copies = [], {}

    def send_row(k, g, count):
        base, w = LATE[k]
        rows, lanes = pl.ds(base, w), pl.ds(g * order, count * order)
        row_copies[k, g] = remote(
            own.at[rows, lanes], right.at[rows, lanes], row_send.at[k, g], row_recv.at[k, g], opposite)

    for g in range(groups):
        for load in loads[g]:
            load.wait()
        rows = []
        for i in range(order // BLK):
            rows.append(jnp.concatenate([
                c_in[g, i * BLK:(i + 1) * BLK, j * BLK:(j + 1) * BLK]
                * mask[g, i, j].astype(jnp.float32).astype(jnp.bfloat16)
                for j in range(width // BLK)], axis=1))
        masked = jnp.concatenate(rows, axis=0)
        top = order // 2
        solved = jnp.concatenate([
            jnp.dot(f_in[g, :top, :top], masked[:top], preferred_element_type=jnp.float32),
            jnp.dot(f_in[g, top:], masked, preferred_element_type=jnp.float32)], axis=0)
        turned = solved.T.astype(jnp.bfloat16)
        lanes = slice(g * order, (g + 1) * order)
        own[:, lanes] = turned
        if g == 0:
            pl.semaphore_wait(barrier, len(peers))
        send_row(0, g, 1)
        for a in range(2):
            for b in range(2):
                at = pl.multiple_of(col * block + a * share, share)
                left[b, pl.ds(at, share), lanes] = turned[(2 * a + b) * share:(2 * a + b + 1) * share]
        mine = left.at[:, pl.ds(pl.multiple_of(col * block, block), block), pl.ds(g * order, order)]
        col_copies.append(remote(mine, mine, col_send.at[g], col_recv.at[g], sibling))
    for k in range(1, len(LATE)):
        send_row(k, 0, groups)

    def column(p):
        return 3 * col if p == 0 else 1 + col

    def level(p, e):
        return lax.rem(column(p) + e, DEPTH)

    def slab(at):
        return pl.ds(pl.multiple_of(at * share, share), share)

    def product(b, p, e):
        rhs = own[pl.ds(pl.multiple_of((col if p == 0 else 1 - col) * block, block), block), :]
        return lax.dot_general(left[b, slab(level(p, e)), :], rhs, NT, preferred_element_type=jnp.float32)

    def late_product(b, p, d):
        base, w = LATE[p]
        return lax.dot_general(left[b, slab(apart[d]), :], right[base:base + w, :], NT,
                               preferred_element_type=jnp.float32)

    x_copies, lx_copies, lz_copies = {}, {}, {}
    place_of = {(p, e): (k, i) for k, (p, es) in enumerate(GROUPS) for i, e in enumerate(es)}
    late_place = {(p, d): (k, i) for k, (p, ds) in enumerate(LATE_GROUPS) for i, d in enumerate(ds)}

    def multiply(k):
        p, es = GROUPS[k]
        for i, e in enumerate(es):
            away[i] = product(1 - x, p, e)
        pack(x_out[k], [away[i] for i in range(len(es))])
        x_copies[k] = remote(x_out[k], x_in[k], x_send.at[k], x_recv.at[k], across)

    def retain(k):
        p, es = GROUPS[k]
        for e in es:
            keep[INDEX[p, e]] = product(x, p, e)

    def take(p, e):
        k, i = place_of[p, e]
        if i == 0:
            x_copies[k].wait_recv()
        me, at = INDEX[p, e], level(p, e)
        differ = lax.rem(z + at, 2) == 1
        copy = remote(z_out.at[me], near_in.at[me], z_send.at[me], near_recv.at[me], (2 * near + x, row, col), differ)
        keep[me] = keep[me] + unpack(x_in[k], i * share, share)

        @pl.when(differ)
        def _():
            pack(z_out.at[me], [keep[me]])
            copy.start()

    def relay(p, e):
        me, at = INDEX[p, e], level(p, e)
        passed = far == at
        copy = remote(z_out.at[me], far_in.at[me], z_send.at[me], far_recv.at[me], (2 * far + x, row, col), passed)

        @pl.when(lax.rem(z + at, 2) == 0)
        def _():
            pltpu.make_async_copy(near_in.at[me], near_in.at[me], near_recv.at[me]).wait()
            keep[me] = keep[me] + unpack(near_in.at[me], 0, share)

        @pl.when(passed)
        def _():
            pack(z_out.at[me], [keep[me]])
            copy.start()

    def show(place, value):
        for c in range(value.shape[1] // LANES):
            out[pl.ds(place + c, share, stride=2 * lines), :] = value[:, c * LANES:(c + 1) * LANES]

    def finish(p, e):
        me, at = INDEX[p, e], level(p, e)
        final = z == at
        copies = []
        if (p, e) in SWAPS:
            s = SWAPS.index((p, e))
            for b in range(2):
                copies.append(remote(
                    swap_out.at[s, b], swap_in.at[lax.rem(at, 2), x],
                    swap_send.at[s, b], swap_recv.at[lax.rem(at, 2), x],
                    (2 * column(p) + b, row, at // 2), final))

        @pl.when(final)
        def _():
            pltpu.make_async_copy(far_in.at[me], far_in.at[me], far_recv.at[me]).wait()
            keep[me] = keep[me] + unpack(far_in.at[me], 0, share)
            if copies:
                flipped = keep[me].T
                for b, copy in enumerate(copies):
                    pack_square(swap_out.at[s, b], flipped[b * share:(b + 1) * share, :])
                    copy.start()
            show(row * lines + (column(p) - 2 * col) * (block // LANES), keep[me])

    def close(l):
        steps = lax.rem(z - (2 * col + l) + DEPTH, DEPTH)

        @pl.when(steps > jnp.where(col == l, 2, 1))
        def _():
            for b in range(2):
                pltpu.make_async_copy(swap_in.at[l, b], swap_in.at[l, b], swap_recv.at[l, b]).wait()
                unpack_square(swap_in.at[l, b], joined, b * share, share)
            show(row * lines + l * (block // LANES), joined[...])

    def gather():
        for copy in col_copies:
            copy.wait_recv()

    def arrive(p):
        for g in range(groups if p == 0 else 1):
            row_copies[p, g].wait_recv()

    def late_multiply(k):
        p, ds = LATE_GROUPS[k]
        w = LATE[p][1]
        for i, d in enumerate(ds):
            away[i, :, 0:w] = late_product(1 - x, p, d)
        pack(lx_out[k], [away[i, :, 0:w] for i in range(len(ds))])
        lx_copies[k] = remote(lx_out[k], lx_in[k], lx_send.at[k], lx_recv.at[k], across)

    def late_retain(p):
        for d in ORDER:
            l_keep[p][d] = late_product(x, p, d)

    def late_take(p, d):
        k, i = late_place[p, d]
        if i == 0:
            lx_copies[k].wait_recv()
        value = l_keep[p][d] + unpack(lx_in[k], i * share, share)
        if d == 0:
            l_keep[p][0] = value
            return
        pack(lz_out[p].at[d], [value])
        lz_copies[p, d] = remote(
            lz_out[p].at[d], lz_in[p].at[d], lz_send.at[p, d], lz_recv.at[p, d], (2 * apart[d] + x, row, col))

    def late_finish(p):
        value = l_keep[p][0]
        for d in ORDER[:-1]:
            lz_copies[p, d].wait_recv()
            value += unpack(lz_in[p].at[d], 0, share)
        show((1 - row) * lines + LATE[p][0] // LANES, value)

    plan = [(multiply, 0), (gather,), (multiply, 1), (multiply, 2), (multiply, 3), (retain, 0), (retain, 1),
            (retain, 2), (retain, 3), (take, 0, 0), (take, 0, 1), (take, 0, 2), (relay, 0, 0), (arrive, 0),
            (late_multiply, 0), (late_multiply, 1), (late_retain, 0), (take, 1, 1), (relay, 0, 1), (relay, 0, 2),
            (finish, 0, 0), (finish, 0, 1), (finish, 0, 2), (late_take, 0, 3), (late_take, 0, 2), (take, 1, 0),
            (relay, 1, 1), (relay, 1, 0), (arrive, 1), (late_multiply, 2), (late_multiply, 3), (late_take, 0, 1),
            (late_take, 0, 0), (late_retain, 1), (late_finish, 0), (finish, 1, 1), (finish, 1, 0), (late_take, 1, 3),
            (arrive, 2), (late_multiply, 4), (late_multiply, 5), (late_take, 1, 2), (late_retain, 2),
            (late_take, 1, 1), (late_take, 1, 0), (late_take, 2, 3), (late_take, 2, 2), (close, 0), (close, 1),
            (arrive, 3), (late_multiply, 6), (late_multiply, 7), (late_multiply, 8), (late_multiply, 9),
            (late_take, 2, 1), (late_take, 2, 0), (late_retain, 3), (late_take, 3, 3), (late_take, 3, 2),
            (late_finish, 1), (late_finish, 2), (late_take, 3, 1), (late_take, 3, 0), (late_finish, 3)]
    for task, *which in plan:
        task(*which)
    for copy, condition in pending:
        if condition is None:
            copy.wait_send()
        else:
            pl.when(condition)(copy.wait_send)


def fused(coupling, factor_inv, block_mask):
    groups, order, width = coupling.shape
    depth, share = groups * order, width // DEPTH
    block, message, count = 2 * share, HEAD + share, len(INDEX)
    square = 2 * HEAD + share + share // 2
    hbm = pl.BlockSpec(memory_space=pl.ANY)
    packets = [pltpu.VMEM((HEAD + share * len(es), block), LINK) for _, es in GROUPS]
    late_packets = [pltpu.VMEM((HEAD + share * len(ds), LATE[p][1]), LINK) for p, ds in LATE_GROUPS]
    sums = [pltpu.VMEM((DEPTH, share, w), jnp.float32) for _, w in LATE]
    messages = [pltpu.VMEM((DEPTH, message, w), LINK) for _, w in LATE]
    dma = pltpu.SemaphoreType.DMA
    tile = pl.pallas_call(
        kernel,
        out_shape=jax.ShapeDtypeStruct((share * 2 * width // LANES, LANES), jnp.float32),
        in_specs=[hbm, hbm, pl.BlockSpec(memory_space=pltpu.SMEM)],
        out_specs=pl.BlockSpec(memory_space=pltpu.VMEM),
        scratch_shapes=[
            pltpu.VMEM((groups, order, width), jnp.bfloat16),
            pltpu.VMEM((groups, order, order), jnp.bfloat16),
            pltpu.VMEM((width, depth), jnp.bfloat16),
            pltpu.VMEM((2, width, depth), jnp.bfloat16),
            pltpu.VMEM((width, depth), jnp.bfloat16),
            pltpu.VMEM((2, share, block), jnp.float32),
            pltpu.VMEM((count, share, block), jnp.float32),
            pltpu.VMEM((share, block), jnp.float32),
            pltpu.VMEM((count, message, block), LINK),
            pltpu.VMEM((count, message, block), LINK),
            pltpu.VMEM((count, message, block), LINK),
            pltpu.VMEM((len(SWAPS), 2, square, LANES), LINK),
            pltpu.VMEM((2, 2, square, LANES), LINK),
            dma((groups, 2)), dma((groups,)), dma((groups,)),
            dma((len(LATE), groups)), dma((len(LATE), groups)),
            dma((len(GROUPS),)), dma((len(GROUPS),)),
            dma((len(LATE_GROUPS),)), dma((len(LATE_GROUPS),)),
            dma((count,)), dma((count,)), dma((count,)),
            dma((len(SWAPS), 2)), dma((2, 2)),
            dma((len(LATE), DEPTH)), dma((len(LATE), DEPTH)),
            *packets, *packets, *late_packets, *late_packets, *sums, *messages, *messages,
        ],
        compiler_params=pltpu.CompilerParams(
            collective_id=0, has_side_effects=True, vmem_limit_bytes=52 * 1024 * 1024),
    )(coupling, factor_inv, block_mask)
    return tile.reshape(1, share, 2, 1, width)


def plain(coupling, factor_inv, block_mask):
    groups, order, width = coupling.shape
    spread = jnp.broadcast_to(
        block_mask[:, :, None, :, None], (groups, order // BLK, BLK, width // BLK, BLK)
    )
    masked = coupling * spread.reshape(groups, order, width).astype(jnp.bfloat16)
    solved = jnp.einsum(
        "snk,skw->snw", factor_inv, masked, preferred_element_type=jnp.float32
    ).astype(jnp.bfloat16)
    left = lax.all_gather(solved, "col", axis=2, tiled=True)
    share = left.shape[2] // lax.axis_size("scen")
    tile = lax.dot_general(
        left,
        lax.all_gather(solved, "row", axis=2, tiled=True),
        (((0, 1), (0, 1)), ((), ())),
        preferred_element_type=jnp.float32,
    )
    summed = lax.psum_scatter(tile, "scen", scatter_dimension=0, tiled=True)
    return summed.reshape(1, share, summed.shape[1] // width, 1, width)


def solution(mesh):
    n, n_row = mesh.shape["scen"], mesh.shape["row"]

    def shards(coupling, factor_inv, block_mask):
        groups, order, width = coupling.shape
        if n == 2 * DEPTH and n_row == 2 and (groups, order, width) == (3, 512, 768):
            return fused(coupling, factor_inv, block_mask)
        return plain(coupling, factor_inv, block_mask)

    in_specs = (
        P("scen", None, ("row", "col")),
        P("scen", None, None),
        P("scen", None, ("row", "col")),
    )
    out_specs = P("row", "scen", None, "col", None)
    return jax.shard_map(shards, mesh=mesh, in_specs=in_specs, out_specs=out_specs, check_vma=False)
```

```python
import functools

import jax
import jax.numpy as jnp
from jax import lax
from jax.experimental import pallas as pl
from jax.experimental.pallas import tpu as pltpu
from jax.sharding import PartitionSpec as P

BLK = 128
LANES = 128
HEAD = 16
LINK = jnp.int16
FINE = 64.0
TOP = 14.9
DEPTH = 4
MESH = pl.DeviceIdType.MESH
NT = (((1,), (1,)), ((), ()))
PIECES = (3, 2)
LATE = ((0, 256), (256, 256), (512, 128), (640, 128))
SWAPS = ((0, 1), (0, 2), (1, 1))
GROUPS = ((0, (0,)), (0, (1, 2)), (1, (1,)), (1, (0,)))
LATE_GROUPS = ((0, (3, 2)), (0, (1, 0)), (1, (3, 2)), (1, (1, 0)), (2, (3, 2)), (2, (1, 0)),
               (3, (3,)), (3, (2,)), (3, (1,)), (3, (0,)))
ORDER = (3, 2, 1, 0)


def power_of(values):
    most = jnp.max(jnp.abs(values[0]), axis=0, keepdims=True)
    for value in values[1:]:
        most = jnp.maximum(most, jnp.max(jnp.abs(value), axis=0, keepdims=True))
    return jnp.ceil(jnp.log2(jnp.maximum(most, 1e-30)) * FINE)


def pack(ref, values):
    power = power_of(values)
    scale = jnp.exp2(TOP - power / FINE)
    ref[0:HEAD, :] = jnp.broadcast_to(power, (HEAD, power.shape[1])).astype(jnp.int32).astype(LINK)
    start = HEAD
    for value in values:
        count = value.shape[0]
        ref[start:start + count, :] = jnp.round(value * scale).astype(jnp.int32).astype(LINK)
        start += count


def unpack(ref, start, count):
    power = ref[0:HEAD, :].astype(jnp.int32).astype(jnp.float32)[0:1, :]
    scaled = ref[HEAD + start:HEAD + start + count, :].astype(jnp.int32).astype(jnp.float32)
    return scaled * jnp.exp2(power / FINE - TOP)


def pack_square(ref, value):
    side = value.shape[0]
    power = power_of([value])
    scaled = jnp.round(value * jnp.exp2(TOP - power / FINE))
    heads = (power[:, :LANES], jnp.concatenate([power[:, LANES:]] * 2, axis=1))
    rest = jnp.concatenate([scaled[:side // 2, LANES:], scaled[side // 2:, LANES:]], axis=1)
    start = 0
    for head, body in zip(heads, (scaled[:, :LANES], rest)):
        ref[start:start + HEAD, :] = jnp.broadcast_to(head, (HEAD, LANES)).astype(jnp.int32).astype(LINK)
        ref[start + HEAD:start + HEAD + body.shape[0], :] = body.astype(jnp.int32).astype(LINK)
        start += HEAD + body.shape[0]


def unpack_square(ref, to, base, side):
    to[:, base:base + LANES] = unpack(ref, 0, side)
    rest = unpack(ref.at[HEAD + side:], 0, side // 2)
    more = side - LANES
    to[0:side // 2, base + LANES:base + side] = rest[:, :more]
    to[side // 2:, base + LANES:base + side] = rest[:, more:]


INDEX = {key: i for i, key in enumerate((p, e) for p, size in enumerate(PIECES) for e in range(size))}


def kernel(coupling, factor, mask, out, c_in, f_in, own, left, right, away, keep, joined,
           z_out, near_in, far_in, swap_out, swap_in,
           in_sem, col_send, col_recv, row_send, row_recv, x_send, x_recv, lx_send, lx_recv,
           z_send, near_recv, far_recv, swap_send, swap_recv, lz_send, lz_recv, *buffers):
    groups, order, width = coupling.shape
    share = width // DEPTH
    block = 2 * share
    lines = width // LANES
    sizes = (len(GROUPS), len(GROUPS), len(LATE_GROUPS), len(LATE_GROUPS), len(LATE), len(LATE), len(LATE))
    parts, start = [], 0
    for size in sizes:
        parts.append(buffers[start:start + size])
        start += size
    x_out, x_in, lx_out, lx_in, l_keep, lz_out, lz_in = parts
    scen, row, col = lax.axis_index("scen"), lax.axis_index("row"), lax.axis_index("col")
    z, x = scen // 2, lax.rem(scen, 2)
    near = z + 1 - 2 * lax.rem(z, 2)
    far = lax.rem(z + 2, DEPTH)
    apart = (z, near, far, DEPTH - 1 - z)
    across = (2 * z + 1 - x, row, col)
    opposite = (scen, 1 - row, col)
    sibling = (scen, row, 1 - col)

    loads = []
    for g in range(groups):
        pair = []
        for src, dst, k in ((coupling, c_in, 0), (factor, f_in, 1)):
            load = pltpu.make_async_copy(src.at[g], dst.at[g], in_sem.at[g, k])
            load.start()
            pair.append(load)
        loads.append(pair)

    barrier = pltpu.get_barrier_semaphore()
    peers = [across, opposite, sibling] + [(2 * level + x, row, col) for level in apart[1:]]
    for peer in peers:
        pl.semaphore_signal(barrier, inc=1, device_id=peer, device_id_type=MESH)

    pending = []

    def remote(src, dst, send_sem, recv_sem, device, condition=None):
        copy = pltpu.make_async_remote_copy(
            src_ref=src, dst_ref=dst, send_sem=send_sem, recv_sem=recv_sem,
            device_id=device, device_id_type=MESH)
        pending.append((copy, condition))
        if condition is None:
            copy.start()
        return copy

    col_copies, row_copies = [], {}

    def send_row(k, g, count):
        base, w = LATE[k]
        rows, lanes = pl.ds(base, w), pl.ds(g * order, count * order)
        row_copies[k, g] = remote(
            own.at[rows, lanes], right.at[rows, lanes], row_send.at[k, g], row_recv.at[k, g], opposite)

    for g in range(groups):
        for load in loads[g]:
            load.wait()
        rows = []
        for i in range(order // BLK):
            rows.append(jnp.concatenate([
                c_in[g, i * BLK:(i + 1) * BLK, j * BLK:(j + 1) * BLK]
                * mask[g, i, j].astype(jnp.float32).astype(jnp.bfloat16)
                for j in range(width // BLK)], axis=1))
        masked = jnp.concatenate(rows, axis=0)
        solved = jnp.concatenate([
            jnp.dot(f_in[g, end - BLK:end, :end], masked[:end], preferred_element_type=jnp.float32)
            for end in range(BLK, order + 1, BLK)], axis=0)
        turned = solved.T.astype(jnp.bfloat16)
        lanes = slice(g * order, (g + 1) * order)
        own[:, lanes] = turned
        if g == 0:
            pl.semaphore_wait(barrier, len(peers))
        send_row(0, g, 1)
        for a in range(2):
            for b in range(2):
                at = pl.multiple_of(col * block + a * share, share)
                left[b, pl.ds(at, share), lanes] = turned[(2 * a + b) * share:(2 * a + b + 1) * share]
        mine = left.at[:, pl.ds(pl.multiple_of(col * block, block), block), pl.ds(g * order, order)]
        col_copies.append(remote(mine, mine, col_send.at[g], col_recv.at[g], sibling))
    for k in range(1, len(LATE)):
        send_row(k, 0, groups)

    def column(p):
        return 3 * col if p == 0 else 1 + col

    def level(p, e):
        return lax.rem(column(p) + e, DEPTH)

    def slab(at):
        return pl.ds(pl.multiple_of(at * share, share), share)

    def product(b, p, e):
        rhs = own[pl.ds(pl.multiple_of((col if p == 0 else 1 - col) * block, block), block), :]
        return lax.dot_general(left[b, slab(level(p, e)), :], rhs, NT, preferred_element_type=jnp.float32)

    def late_product(b, p, d):
        base, w = LATE[p]
        return lax.dot_general(left[b, slab(apart[d]), :], right[base:base + w, :], NT,
                               preferred_element_type=jnp.float32)

    x_copies, lx_copies, lz_copies = {}, {}, {}
    place_of = {(p, e): (k, i) for k, (p, es) in enumerate(GROUPS) for i, e in enumerate(es)}
    late_place = {(p, d): (k, i) for k, (p, ds) in enumerate(LATE_GROUPS) for i, d in enumerate(ds)}

    def multiply(k):
        p, es = GROUPS[k]
        for i, e in enumerate(es):
            away[i] = product(1 - x, p, e)
        pack(x_out[k], [away[i] for i in range(len(es))])
        x_copies[k] = remote(x_out[k], x_in[k], x_send.at[k], x_recv.at[k], across)

    def retain(k):
        p, es = GROUPS[k]
        for e in es:
            keep[INDEX[p, e]] = product(x, p, e)

    def take(p, e):
        k, i = place_of[p, e]
        if i == 0:
            x_copies[k].wait_recv()
        me, at = INDEX[p, e], level(p, e)
        differ = lax.rem(z + at, 2) == 1
        copy = remote(z_out.at[me], near_in.at[me], z_send.at[me], near_recv.at[me], (2 * near + x, row, col), differ)
        keep[me] = keep[me] + unpack(x_in[k], i * share, share)

        @pl.when(differ)
        def _():
            pack(z_out.at[me], [keep[me]])
            copy.start()

    def relay(p, e):
        me, at = INDEX[p, e], level(p, e)
        passed = far == at
        copy = remote(z_out.at[me], far_in.at[me], z_send.at[me], far_recv.at[me], (2 * far + x, row, col), passed)

        @pl.when(lax.rem(z + at, 2) == 0)
        def _():
            pltpu.make_async_copy(near_in.at[me], near_in.at[me], near_recv.at[me]).wait()
            keep[me] = keep[me] + unpack(near_in.at[me], 0, share)

        @pl.when(passed)
        def _():
            pack(z_out.at[me], [keep[me]])
            copy.start()

    def show(place, value):
        for c in range(value.shape[1] // LANES):
            out[pl.ds(place + c, share, stride=2 * lines), :] = value[:, c * LANES:(c + 1) * LANES]

    def finish(p, e):
        me, at = INDEX[p, e], level(p, e)
        final = z == at
        copies = []
        if (p, e) in SWAPS:
            s = SWAPS.index((p, e))
            for b in range(2):
                copies.append(remote(
                    swap_out.at[s, b], swap_in.at[lax.rem(at, 2), x],
                    swap_send.at[s, b], swap_recv.at[lax.rem(at, 2), x],
                    (2 * column(p) + b, row, at // 2), final))

        @pl.when(final)
        def _():
            pltpu.make_async_copy(far_in.at[me], far_in.at[me], far_recv.at[me]).wait()
            keep[me] = keep[me] + unpack(far_in.at[me], 0, share)
            if copies:
                flipped = keep[me].T
                for b, copy in enumerate(copies):
                    pack_square(swap_out.at[s, b], flipped[b * share:(b + 1) * share, :])
                    copy.start()
            show(row * lines + (column(p) - 2 * col) * (block // LANES), keep[me])

    def close(l):
        steps = lax.rem(z - (2 * col + l) + DEPTH, DEPTH)

        @pl.when(steps > jnp.where(col == l, 2, 1))
        def _():
            for b in range(2):
                pltpu.make_async_copy(swap_in.at[l, b], swap_in.at[l, b], swap_recv.at[l, b]).wait()
                unpack_square(swap_in.at[l, b], joined, b * share, share)
            show(row * lines + l * (block // LANES), joined[...])

    def gather():
        for copy in col_copies:
            copy.wait_recv()

    def arrive(p):
        for g in range(groups if p == 0 else 1):
            row_copies[p, g].wait_recv()

    def late_multiply(k):
        p, ds = LATE_GROUPS[k]
        w = LATE[p][1]
        for i, d in enumerate(ds):
            away[i, :, 0:w] = late_product(1 - x, p, d)
        pack(lx_out[k], [away[i, :, 0:w] for i in range(len(ds))])
        lx_copies[k] = remote(lx_out[k], lx_in[k], lx_send.at[k], lx_recv.at[k], across)

    def late_retain(p):
        for d in ORDER:
            l_keep[p][d] = late_product(x, p, d)

    def late_take(p, d):
        k, i = late_place[p, d]
        if i == 0:
            lx_copies[k].wait_recv()
        value = l_keep[p][d] + unpack(lx_in[k], i * share, share)
        if d == 0:
            l_keep[p][0] = value
            return
        pack(lz_out[p].at[d], [value])
        lz_copies[p, d] = remote(
            lz_out[p].at[d], lz_in[p].at[d], lz_send.at[p, d], lz_recv.at[p, d], (2 * apart[d] + x, row, col))

    def late_finish(p):
        value = l_keep[p][0]
        for d in ORDER[:-1]:
            lz_copies[p, d].wait_recv()
            value += unpack(lz_in[p].at[d], 0, share)
        show((1 - row) * lines + LATE[p][0] // LANES, value)

    plan = [(multiply, 0), (gather,), (multiply, 1), (multiply, 2), (multiply, 3), (retain, 0), (retain, 1),
            (retain, 2), (retain, 3), (take, 0, 0), (take, 0, 1), (take, 0, 2), (relay, 0, 0), (arrive, 0),
            (late_multiply, 0), (late_multiply, 1), (late_retain, 0), (take, 1, 1), (relay, 0, 1), (relay, 0, 2),
            (finish, 0, 0), (finish, 0, 1), (finish, 0, 2), (late_take, 0, 3), (late_take, 0, 2), (take, 1, 0),
            (relay, 1, 1), (relay, 1, 0), (arrive, 1), (late_multiply, 2), (late_multiply, 3), (late_take, 0, 1),
            (late_take, 0, 0), (late_retain, 1), (late_finish, 0), (finish, 1, 1), (finish, 1, 0), (late_take, 1, 3),
            (arrive, 2), (late_multiply, 4), (late_multiply, 5), (late_take, 1, 2), (late_retain, 2),
            (late_take, 1, 1), (late_take, 1, 0), (late_take, 2, 3), (late_take, 2, 2), (close, 0), (close, 1),
            (arrive, 3), (late_multiply, 6), (late_multiply, 7), (late_multiply, 8), (late_multiply, 9),
            (late_take, 2, 1), (late_take, 2, 0), (late_retain, 3), (late_take, 3, 3), (late_take, 3, 2),
            (late_finish, 1), (late_finish, 2), (late_take, 3, 1), (late_take, 3, 0), (late_finish, 3)]
    for task, *which in plan:
        task(*which)
    for copy, condition in pending:
        if condition is None:
            copy.wait_send()
        else:
            pl.when(condition)(copy.wait_send)


def fused(coupling, factor_inv, block_mask):
    groups, order, width = coupling.shape
    depth, share = groups * order, width // DEPTH
    block, message, count = 2 * share, HEAD + share, len(INDEX)
    square = 2 * HEAD + share + share // 2
    hbm = pl.BlockSpec(memory_space=pl.ANY)
    packets = [pltpu.VMEM((HEAD + share * len(es), block), LINK) for _, es in GROUPS]
    late_packets = [pltpu.VMEM((HEAD + share * len(ds), LATE[p][1]), LINK) for p, ds in LATE_GROUPS]
    sums = [pltpu.VMEM((DEPTH, share, w), jnp.float32) for _, w in LATE]
    messages = [pltpu.VMEM((DEPTH, message, w), LINK) for _, w in LATE]
    dma = pltpu.SemaphoreType.DMA
    tile = pl.pallas_call(
        kernel,
        out_shape=jax.ShapeDtypeStruct((share * 2 * width // LANES, LANES), jnp.float32),
        in_specs=[hbm, hbm, pl.BlockSpec(memory_space=pltpu.SMEM)],
        out_specs=pl.BlockSpec(memory_space=pltpu.VMEM),
        scratch_shapes=[
            pltpu.VMEM((groups, order, width), jnp.bfloat16),
            pltpu.VMEM((groups, order, order), jnp.bfloat16),
            pltpu.VMEM((width, depth), jnp.bfloat16),
            pltpu.VMEM((2, width, depth), jnp.bfloat16),
            pltpu.VMEM((width, depth), jnp.bfloat16),
            pltpu.VMEM((2, share, block), jnp.float32),
            pltpu.VMEM((count, share, block), jnp.float32),
            pltpu.VMEM((share, block), jnp.float32),
            pltpu.VMEM((count, message, block), LINK),
            pltpu.VMEM((count, message, block), LINK),
            pltpu.VMEM((count, message, block), LINK),
            pltpu.VMEM((len(SWAPS), 2, square, LANES), LINK),
            pltpu.VMEM((2, 2, square, LANES), LINK),
            dma((groups, 2)), dma((groups,)), dma((groups,)),
            dma((len(LATE), groups)), dma((len(LATE), groups)),
            dma((len(GROUPS),)), dma((len(GROUPS),)),
            dma((len(LATE_GROUPS),)), dma((len(LATE_GROUPS),)),
            dma((count,)), dma((count,)), dma((count,)),
            dma((len(SWAPS), 2)), dma((2, 2)),
            dma((len(LATE), DEPTH)), dma((len(LATE), DEPTH)),
            *packets, *packets, *late_packets, *late_packets, *sums, *messages, *messages,
        ],
        compiler_params=pltpu.CompilerParams(
            collective_id=0, has_side_effects=True, vmem_limit_bytes=52 * 1024 * 1024),
    )(coupling, factor_inv, block_mask)
    return tile.reshape(1, share, 2, 1, width)


def plain(coupling, factor_inv, block_mask):
    groups, order, width = coupling.shape
    spread = jnp.broadcast_to(
        block_mask[:, :, None, :, None], (groups, order // BLK, BLK, width // BLK, BLK)
    )
    masked = coupling * spread.reshape(groups, order, width).astype(jnp.bfloat16)
    solved = jnp.einsum(
        "snk,skw->snw", factor_inv, masked, preferred_element_type=jnp.float32
    ).astype(jnp.bfloat16)
    left = lax.all_gather(solved, "col", axis=2, tiled=True)
    share = left.shape[2] // lax.axis_size("scen")
    tile = lax.dot_general(
        left,
        lax.all_gather(solved, "row", axis=2, tiled=True),
        (((0, 1), (0, 1)), ((), ())),
        preferred_element_type=jnp.float32,
    )
    summed = lax.psum_scatter(tile, "scen", scatter_dimension=0, tiled=True)
    return summed.reshape(1, share, summed.shape[1] // width, 1, width)


def solution(mesh):
    n, n_row = mesh.shape["scen"], mesh.shape["row"]

    def shards(coupling, factor_inv, block_mask):
        groups, order, width = coupling.shape
        if n == 2 * DEPTH and n_row == 2 and (groups, order, width) == (3, 512, 768):
            return fused(coupling, factor_inv, block_mask)
        return plain(coupling, factor_inv, block_mask)

    in_specs = (
        P("scen", None, ("row", "col")),
        P("scen", None, None),
        P("scen", None, ("row", "col")),
    )
    out_specs = P("row", "scen", None, "col", None)
    return jax.shard_map(shards, mesh=mesh, in_specs=in_specs, out_specs=out_specs, check_vma=False)
```
